32 devices in a mesh: grp: 2 (over y), tm: 4 (over z), mod: 4 (over x, core).
Axes of the slice: x: 2, y: 2, z: 4, core: 2. Of those that a mesh axis runs over, the one named last changes fastest.
Arguments:
- phase: float32 [16, 512, 128], P(('grp', 'tm'), 'mod'), parts along dimension 0, may hold values from -4 to 4
- direction: float32 [16, 512, 128], P(('grp', 'tm'), 'mod'), parts along dimension 0, may hold values from -16 to 16
- pupil_mask: int32 [512, 128], replicated, may hold values 0 or 1
- mod_tilts: int32 [4], P('mod'), may hold values from -8 to 8
- wind_codes: int32 [1024, 128], P('grp'), parts along dimension 0, may hold values from 0 to 15
- noise_weight: float32 [16, 1024, 128], P(('grp', 'tm')), parts along dimension 0, may hold values from 0.075 to 0.75
Outputs:
- hess_vec: float32 [16, 512, 128], P(('grp', 'tm'), 'mod'), parts along dimension 0
- curvature: float32 [2], P('grp'), parts along dimension 0
The draws below stay inside these ranges and needn't reach their ends.
There are 2 independent parts, one for each index of `grp`. The reference program is written for one: setup_inputs(seed, part) draws one part's arguments, and reference() takes and returns one part's arrays. A program takes and returns all parts, laid end to end along the dimension named above; an argument that names none is the same for every part. Nothing has to cross between parts.
All inputs are finite; a program needn't handle non-finite values.
Results may differ from the reference program's by a relative error of at most 0.0003.
Values sent between devices are 32-bit elements; how exact they have to be, the bound alone decides.
A program may use at most 64 MiB of HBM per device.

```python
import math
import jax
import jax.numpy as jnp
from jax import lax

PUPIL = 512
NPIX = 1024
ROWS = 128
FRAMES = 8
MODS = 4
MODR = 8


def draw_direction(key, part):
    shape = (FRAMES, PUPIL, ROWS)
    frame_pos = lax.broadcasted_iota(jnp.float32, shape, 0) / (FRAMES - 1)
    pixel_pos = lax.broadcasted_iota(jnp.float32, shape, 1) / (PUPIL - 1)
    base = jax.random.truncated_normal(key, -4.0, 4.0, shape, jnp.float32)
    ramp = jnp.exp(0.5 * jnp.log(3.0) * (frame_pos + pixel_pos))
    return base * ramp


def touch_ends(drawn, rng, low, top_value):
    longest = drawn.shape.index(max(drawn.shape))
    spots = []
    for shift in (0, 1):
        where = [jax.random.randint(jax.random.fold_in(rng, axis), (), 0, length) for axis, length in enumerate(drawn.shape)]
        where[longest] = (where[longest] + shift) % drawn.shape[longest]
        spots.append(tuple(where))
    return drawn.at[spots[0]].set(low).at[spots[1]].set(top_value)


def level_of(stream_key, dims, shards, least, top_value):
    level = 1.0
    for position, parts in shards:
        draws = jax.random.uniform(jax.random.fold_in(jax.random.fold_in(stream_key, 6), position), (parts,), jnp.float32, least / len(shards), top_value / len(shards))
        level = level * jnp.repeat(jnp.exp(draws), dims[position] // parts).reshape((-1,) + (1,) * (len(dims) - 1 - position))
    return level


def scatter_about(rng, dims, scale, most, shards=(), held_as=jnp.bfloat16):
    drawn = jax.random.normal(rng, dims, jnp.float32) * scale
    if len(shards) > 0:
        drawn = level_of(rng, dims, shards, -0.22, 0.18) * drawn
    return jnp.clip(drawn, min=-most, max=most).astype(held_as)


def setup_inputs(seed: int = 0, part: int = 0) -> dict:
    keys = jax.random.split(jax.random.key(seed), 7)
    own_keys = jax.random.split(jax.random.fold_in(keys[6], part), 7)
    return {
        "phase": scatter_about(own_keys[0], (FRAMES, PUPIL, ROWS), 1.0, 4.0, ((0, 4), (1, 4)), jnp.float32),
        "direction": draw_direction(jax.random.fold_in(jax.random.fold_in(keys[6], part), 71), part),
        "pupil_mask": touch_ends((jax.random.randint(keys[2], (PUPIL, ROWS), 0, 8) < 7).astype(jnp.int32), jax.random.fold_in(keys[2], 1), 0, 1),
        "mod_tilts": touch_ends(jax.random.randint(keys[3], (MODS,), -MODR, MODR + 1), jax.random.fold_in(keys[3], 1), -MODR, MODR).astype(jnp.int32),
        "wind_codes": touch_ends(jax.random.randint(own_keys[4], (PUPIL, ROWS), 0, 16), jax.random.fold_in(own_keys[4], 1), 0, 15).astype(jnp.int32),
        "noise_weight": jnp.clip(jnp.exp(math.log(0.75) - 2.3025851 * jax.random.uniform(own_keys[5], (FRAMES, NPIX, ROWS), jnp.float32) ** level_of(own_keys[5], (FRAMES, NPIX, ROWS), ((0, 4),), -0.2, 0.2)), 0.075, 0.75),
    }


def roof_mask(length, shift_bins):
    freq_index = jnp.arange(length, dtype=jnp.int32)
    signed_freq = jnp.where(freq_index < length // 2, freq_index, freq_index - length)
    turn_counts = (shift_bins * jnp.abs(signed_freq)) % length
    angles = (-2.0 * jnp.pi / length) * turn_counts.astype(jnp.float32)
    return jnp.cos(angles), jnp.sin(angles)


def apply_pyramid(field_real, field_imag, gain_real, gain_imag):
    field = lax.complex(field_real, field_imag)
    spectrum = jnp.fft.fft(field, axis=1)
    gain = lax.complex(gain_real, gain_imag)[None, :, None]
    result = jnp.fft.ifft(spectrum * gain, axis=1)
    return jnp.real(result), jnp.imag(result)


def reference(phase, direction, pupil_mask, mod_tilts, wind_codes, noise_weight):
    frames, pupil_width, row_count = phase.shape
    line_length = 2 * pupil_width
    quarter = pupil_width // 2
    amplitude = pupil_mask.astype(jnp.float32)
    positions = quarter + jnp.arange(pupil_width, dtype=jnp.int32)
    gain_real, gain_imag = roof_mask(line_length, quarter)
    margins = ((0, 0), (quarter, quarter), (0, 0))

    def fields(tilt):
        turn_counts = (tilt * positions) % line_length
        angles = phase + ((2.0 * jnp.pi / line_length) * turn_counts.astype(jnp.float32))[None, :, None]
        return amplitude * jnp.cos(angles), amplitude * jnp.sin(angles)

    def forward(carry, tilt):
        field_real, field_imag = fields(tilt)
        image_real, image_imag = apply_pyramid(jnp.pad(field_real, margins), jnp.pad(field_imag, margins), gain_real, gain_imag)
        push_real, push_imag = apply_pyramid(jnp.pad(-field_imag * direction, margins), jnp.pad(field_real * direction, margins), gain_real, gain_imag)
        return carry + 2.0 * (image_real * push_real + image_imag * push_imag), None

    signal, _ = lax.scan(forward, jnp.zeros((frames, line_length, row_count), jnp.float32), mod_tilts)
    weighted = noise_weight * signal

    def backward(carry, tilt):
        field_real, field_imag = fields(tilt)
        image_real, image_imag = apply_pyramid(jnp.pad(field_real, margins), jnp.pad(field_imag, margins), gain_real, gain_imag)
        back_real, back_imag = apply_pyramid(weighted * image_real, weighted * image_imag, gain_real, -gain_imag)
        back_real = back_real[:, quarter:quarter + pupil_width]
        back_imag = back_imag[:, quarter:quarter + pupil_width]
        return carry - 2.0 * (field_imag * back_real - field_real * back_imag), None

    data_grad, _ = lax.scan(backward, jnp.zeros((frames, pupil_width, row_count), jnp.float32), mod_tilts)

    frac_x = ((wind_codes % 4).astype(jnp.float32) + 0.5) / 4.0
    frac_r = ((wind_codes // 4).astype(jnp.float32) + 0.5) / 4.0
    stay_stay = (1.0 - frac_x) * (1.0 - frac_r)
    ahead_stay = frac_x * (1.0 - frac_r)
    stay_ahead = (1.0 - frac_x) * frac_r
    ahead_ahead = frac_x * frac_r

    def advect(field):
        next_x = jnp.pad(field[:, 1:, :], ((0, 0), (0, 1), (0, 0)))
        next_r = jnp.pad(field[:, :, 1:], ((0, 0), (0, 0), (0, 1)))
        next_both = jnp.pad(field[:, 1:, 1:], ((0, 0), (0, 1), (0, 1)))
        return stay_stay * field + ahead_stay * next_x + stay_ahead * next_r + ahead_ahead * next_both

    def advect_adjoint(field):
        part_one = stay_stay * field
        part_two = jnp.pad((ahead_stay * field)[:, :-1, :], ((0, 0), (1, 0), (0, 0)))
        part_three = jnp.pad((stay_ahead * field)[:, :, :-1], ((0, 0), (0, 0), (1, 0)))
        part_four = jnp.pad((ahead_ahead * field)[:, :-1, :-1], ((0, 0), (1, 0), (1, 0)))
        return part_one + part_two + part_three + part_four

    flow = direction[1:] - advect(direction[:-1])
    prior = jnp.pad(flow, ((1, 0), (0, 0), (0, 0))) - jnp.pad(advect_adjoint(flow), ((0, 1), (0, 0), (0, 0)))
    hess_vec = data_grad + prior
    curvature = (jnp.sum(direction * hess_vec) / float(frames * pupil_width * row_count)).reshape(1)
    return hess_vec, curvature
```

```python
import functools

import jax
import jax.numpy as jnp
import numpy as np
from jax import lax
from jax.experimental import pallas as pl
from jax.experimental.pallas import tpu as pltpu
from jax.sharding import PartitionSpec as P

HIGHEST = lax.Precision.HIGHEST


def with_halo(cells, sides, width):
    for axis, dim in sides:
        count = lax.axis_size(axis)
        ends = count - 1
        head = lax.slice_in_dim(cells, 0, width, axis=dim)
        tail = lax.slice_in_dim(cells, cells.shape[dim] - width, cells.shape[dim], axis=dim)
        cells = jnp.concatenate(
            [
                lax.ppermute(tail, axis, [(i, (i + 1) % count) for i in range(ends)]),
                cells,
                lax.ppermute(head, axis, [((i + 1) % count, i) for i in range(ends)]),
            ],
            axis=dim,
        )
    return cells


def square_table(count, orient):
    index_range = jnp.arange(count, dtype=jnp.int32)
    turn_counts = index_range[:, None] * index_range[None, :] % count
    angles = orient * 2.0 * jnp.pi / count * turn_counts.astype(jnp.float32)
    return (jnp.cos(angles), jnp.sin(angles))


def complex_mix(form, table_real, table_imag, field_real, field_imag):
    real_real = jnp.einsum(form, table_real, field_real, precision=HIGHEST)
    imag_imag = jnp.einsum(form, table_imag, field_imag, precision=HIGHEST)
    real_imag = jnp.einsum(form, table_real, field_imag, precision=HIGHEST)
    imag_real = jnp.einsum(form, table_imag, field_real, precision=HIGHEST)
    return (real_real - imag_imag, real_imag + imag_real)


def transform(field_real, field_imag, orient):
    batch_size, length, row_count = field_real.shape
    outer_size = 32
    inner_size = length // outer_size
    first_real, first_imag = square_table(outer_size, orient)
    second_real, second_imag = square_table(inner_size, orient)
    turn_counts = (
        jnp.arange(outer_size, dtype=jnp.int32)[:, None]
        * jnp.arange(inner_size, dtype=jnp.int32)[None, :]
        % length
    )
    angles = orient * 2.0 * jnp.pi / length * turn_counts.astype(jnp.float32)
    twist_real = jnp.cos(angles)[None, :, :, None]
    twist_imag = jnp.sin(angles)[None, :, :, None]
    shaped_real = field_real.reshape(batch_size, outer_size, inner_size, row_count)
    shaped_imag = field_imag.reshape(batch_size, outer_size, inner_size, row_count)
    section_real, section_imag = complex_mix(
        "kn,bnmr->bkmr", first_real, first_imag, shaped_real, shaped_imag
    )
    turned_real = section_real * twist_real - section_imag * twist_imag
    turned_imag = section_real * twist_imag + section_imag * twist_real
    final_real, final_imag = complex_mix(
        "dm,bkmr->bdkr", second_real, second_imag, turned_real, turned_imag
    )
    return (
        final_real.reshape(batch_size, length, row_count),
        final_imag.reshape(batch_size, length, row_count),
    )


def roof_mask(length, shift_bins):
    freq_index = jnp.arange(length, dtype=jnp.int32)
    signed_freq = jnp.where(freq_index < length // 2, freq_index, freq_index - length)
    turn_counts = shift_bins * jnp.abs(signed_freq) % length
    angles = -2.0 * jnp.pi / length * turn_counts.astype(jnp.float32)
    return (jnp.cos(angles), jnp.sin(angles))


def pyramid(field_real, field_imag, gain_real, gain_imag):
    spectrum_real, spectrum_imag = transform(field_real, field_imag, -1.0)
    column_real = gain_real[None, :, None]
    column_imag = gain_imag[None, :, None]
    masked_real = spectrum_real * column_real - spectrum_imag * column_imag
    masked_imag = spectrum_real * column_imag + spectrum_imag * column_real
    back_real, back_imag = transform(masked_real, masked_imag, 1.0)
    inverse_length = 1.0 / field_real.shape[1]
    return (back_real * inverse_length, back_imag * inverse_length)


def row_ahead(field):
    return jnp.pad(field[:, :, 1:], ((0, 0), (0, 0), (0, 1)))


def row_behind(field):
    return jnp.pad(field[:, :, :-1], ((0, 0), (0, 0), (1, 0)))


def flow_terms(extended, frac_x, frac_r, first_frame, total_frames, first_pixel):
    frames_ext, width_ext, row_count = extended.shape
    frames_dev = frames_ext - 2
    near_x = jnp.pad(frac_x, ((1, 0), (0, 0)))
    near_r = jnp.pad(frac_r, ((1, 0), (0, 0)))
    stay_stay = (1.0 - near_x) * (1.0 - near_r)
    ahead_stay = near_x * (1.0 - near_r)
    stay_ahead = (1.0 - near_x) * near_r
    ahead_ahead = near_x * near_r
    base_cells = extended[:, :-1, :]
    ahead_cells = extended[:, 1:, :]
    moved = (
        stay_stay * base_cells
        + ahead_stay * ahead_cells
        + stay_ahead * row_ahead(base_cells)
        + ahead_ahead * row_ahead(ahead_cells)
    )
    flow = extended[1:, :-1, :] - moved[:-1]
    frame_ids = first_frame - 1 + lax.broadcasted_iota(jnp.int32, flow.shape, 0)
    pixel_ids = first_pixel - 1 + lax.broadcasted_iota(jnp.int32, flow.shape, 1)
    valid = (frame_ids >= 0) & (frame_ids <= total_frames - 2) & (pixel_ids >= 0)
    flow = jnp.where(valid, flow, 0.0)
    spread = (
        (stay_stay * flow)[:, 1:]
        + (ahead_stay * flow)[:, :-1]
        + row_behind((stay_ahead * flow)[:, 1:] + (ahead_ahead * flow)[:, :-1])
    )
    prior = flow[:frames_dev, 1:] - spread[1:]
    return (prior, flow[1:, 1:])


def forward_pass(full_phase, full_direction, tilts, amplitude, gain_real, gain_imag):
    frames_dev, pupil_width, row_count = full_phase.shape
    line_length = 2 * pupil_width
    quarter = pupil_width // 2
    local_points = tilts.shape[0]
    positions = quarter + jnp.arange(pupil_width, dtype=jnp.int32)
    tilt_turns = tilts[:, None] * positions[None, :] % line_length
    tilt_angles = 2.0 * jnp.pi / line_length * tilt_turns.astype(jnp.float32)
    angles = full_phase[None] + tilt_angles[:, None, :, None]
    field_real = amplitude * jnp.cos(angles)
    field_imag = amplitude * jnp.sin(angles)
    margins = ((0, 0), (quarter, quarter), (0, 0))
    line_batch = local_points * frames_dev

    def padded_lines(field):
        return jnp.pad(field.reshape(line_batch, pupil_width, row_count), margins)

    image_real, image_imag = pyramid(
        padded_lines(field_real), padded_lines(field_imag), gain_real, gain_imag
    )
    push_real, push_imag = pyramid(
        padded_lines(-field_imag * full_direction),
        padded_lines(field_real * full_direction),
        gain_real,
        gain_imag,
    )
    signal_terms = (2.0 * (image_real * push_real + image_imag * push_imag)).reshape(
        local_points, frames_dev, line_length, row_count
    )
    return (field_real, field_imag, image_real, image_imag, jnp.sum(signal_terms, axis=0))


def backward_pass(
    field_real, field_imag, image_real, image_imag, weighted_full, gain_real, gain_imag
):
    local_points, frames_dev, pupil_width, row_count = field_real.shape
    line_length = 2 * pupil_width
    quarter = pupil_width // 2
    line_batch = local_points * frames_dev
    image_shaped_real = image_real.reshape(local_points, frames_dev, line_length, row_count)
    image_shaped_imag = image_imag.reshape(local_points, frames_dev, line_length, row_count)
    source_real = (weighted_full[None] * image_shaped_real).reshape(
        line_batch, line_length, row_count
    )
    source_imag = (weighted_full[None] * image_shaped_imag).reshape(
        line_batch, line_length, row_count
    )
    back_real, back_imag = pyramid(source_real, source_imag, gain_real, -gain_imag)
    back_real = back_real[:, quarter : quarter + pupil_width].reshape(
        local_points, frames_dev, pupil_width, row_count
    )
    back_imag = back_imag[:, quarter : quarter + pupil_width].reshape(
        local_points, frames_dev, pupil_width, row_count
    )
    return -2.0 * jnp.sum(field_imag * back_real - field_real * back_imag, axis=0)


def per_device(phase, direction, pupil_mask, mod_tilts, wind_codes, noise_weight):
    frames_dev, shard_width, row_count = phase.shape
    mod_count = lax.axis_size("mod")
    pupil_width = shard_width * mod_count
    line_length = 2 * pupil_width
    quarter = pupil_width // 2
    mod_index = lax.axis_index("mod")
    first_frame = lax.axis_index("tm") * frames_dev
    total_frames = frames_dev * lax.axis_size("tm")
    first_pixel = mod_index * shard_width
    frac_x = ((wind_codes % 4).astype(jnp.float32) + 0.5) / 4.0
    frac_r = ((wind_codes // 4).astype(jnp.float32) + 0.5) / 4.0
    gain_real, gain_imag = roof_mask(line_length, quarter)
    rimmed = with_halo(direction, (("tm", 0),), 1)
    full_phase, full_rim = (
        lax.all_gather(phase, "mod", axis=1, tiled=True),
        lax.all_gather(rimmed, "mod", axis=1, tiled=True),
    )
    full_direction = full_rim[1:-1]
    extended = jnp.pad(full_rim, ((0, 0), (1, 1), (0, 0)))
    prior_lines, flow_lines = flow_terms(extended, frac_x, frac_r, first_frame, total_frames, 0)
    prior = lax.dynamic_slice_in_dim(prior_lines, first_pixel, shard_width, 1)
    amplitude = pupil_mask.astype(jnp.float32)
    field_real, field_imag, image_real, image_imag, signal_local = forward_pass(
        full_phase, full_direction, mod_tilts, amplitude, gain_real, gain_imag
    )
    signal_full = lax.psum(signal_local, "mod")
    weighted_used = noise_weight * signal_full
    grad_lines = backward_pass(
        field_real, field_imag, image_real, image_imag, weighted_used, gain_real, gain_imag
    )
    grad_own = lax.psum_scatter(grad_lines, "mod", scatter_dimension=1, tiled=True)
    hess_vec = grad_own + prior
    curvature_total = lax.psum(jnp.sum(direction * hess_vec), ("tm", "mod"))
    entry_count = float(total_frames * pupil_width * row_count)
    curvature = (curvature_total / entry_count).reshape(1)
    return (hess_vec, curvature)


TILE = 16
HALO = 8


def coupling_tables(pupil_width, pieces):
    per_piece = pupil_width // pieces
    order = [
        np.concatenate([pieces * np.arange(per_piece) + j for j in range(parity, pieces, 2)])
        for parity in (0, 1)
    ]
    tables = []
    for source in (0, 1):
        gap = order[1 - source][:, None] - order[source][None, :]
        exact = -1.0 / (pupil_width * np.sin(np.pi * gap / pupil_width))
        high = exact.astype(jnp.bfloat16)
        low = (exact - high.astype(np.float64)).astype(jnp.bfloat16)
        tables.append(np.concatenate([high, high, low], axis=1))
    return np.stack(tables)


def cos_sin(angle):
    turns = jnp.round(angle * np.float32(2.0 / np.pi))
    rest = angle - turns * np.float32(1.5703125)
    rest = rest - turns * np.float32(4.837512969970703125e-4)
    rest = rest - turns * np.float32(7.54978995489188216e-8)
    square = rest * rest
    sine = rest + rest * square * (
        np.float32(-1.6666654611e-1)
        + square * (np.float32(8.3321608736e-3) + square * np.float32(-1.9515295891e-4))
    )
    cosine = (
        1.0
        - 0.5 * square
        + square
        * square
        * (
            np.float32(4.166664568298827e-2)
            + square * (np.float32(-1.388731625493765e-3) + square * np.float32(2.443315711809948e-5))
        )
    )
    quarter = turns.astype(jnp.int32)
    swap = (quarter & 1) == 1
    out_cos = jnp.where(swap, sine, cosine)
    out_sin = jnp.where(swap, cosine, sine)
    out_cos = jnp.where(((quarter + 1) & 2) == 2, -out_cos, out_cos)
    out_sin = jnp.where((quarter & 2) == 2, -out_sin, out_sin)
    return out_cos, out_sin


def split(value):
    high = value.astype(jnp.bfloat16)
    return high, (value - high.astype(jnp.float32)).astype(jnp.bfloat16)


def fused_kernel(
    counts,
    phase,
    direction,
    tilts,
    mask_hbm,
    wind_hbm,
    noise_hbm,
    table_hbm,
    out,
    curvature,
    send_lines,
    lines,
    send_tilt,
    tilt_tiles,
    extended,
    mask,
    wind,
    noise,
    table,
    packed_mask,
    packed_noise,
    turn,
    field,
    operand,
    image,
    push,
    dir_wide,
    bent,
    prior,
    near,
    send_grad,
    grads,
    parts,
    local_sem,
    line_send,
    line_recv,
    halo_send,
    halo_recv,
    grad_send,
    grad_recv,
    part_send,
    part_recv,
):
    tm_count, mod_count = counts
    frames, width, rows = phase.shape
    chunks = mod_count // frames
    chunk = rows // chunks
    pieces = chunks
    sub = width // pieces
    pupil = width * mod_count
    length = 2 * pupil
    packed_rows = pupil // pieces
    half = pupil // 2
    groups = mod_count // pieces
    lanes = groups * rows
    tm = lax.axis_index("tm")
    mod = lax.axis_index("mod")
    own_frame = mod // chunks
    own_chunk = mod % chunks

    copies = [
        pltpu.make_async_copy(noise_hbm.at[own_frame], noise, local_sem.at[0]),
        pltpu.make_async_copy(mask_hbm, mask, local_sem.at[1]),
        pltpu.make_async_copy(wind_hbm, wind, local_sem.at[2]),
        pltpu.make_async_copy(table_hbm, table, local_sem.at[3]),
    ]

    barrier = pltpu.get_barrier_semaphore()
    peers = [
        (a, b) for a in range(tm_count) for b in range(mod_count) if (a, b) != (0, 0)
    ]

    def peer(a, b):
        return {"tm": (tm + a) % tm_count, "mod": (mod + b) % mod_count}

    for a, b in peers:
        pl.semaphore_signal(
            barrier, inc=1, device_id=peer(a, b), device_id_type=pl.DeviceIdType.MESH
        )
    for copy in copies:
        copy.start()

    lane_group = lax.broadcasted_iota(jnp.int32, (TILE, rows), 1) // chunk

    def at_lanes(values):
        out_value = values[0]
        for j in range(1, len(values)):
            out_value = jnp.where(lane_group[: out_value.shape[0]] == j, values[j], out_value)
        return out_value

    def turned(value, amount):
        if isinstance(amount, int):
            amount = amount % rows
            if amount == 0:
                return value
        return pltpu.roll(value, amount, 1)

    def widened(value):
        shifts = [turned(value, s * chunk) for s in range(pieces)]
        return [
            at_lanes([shifts[(m - j) % pieces] for m in range(pieces)]) for j in range(pieces)
        ]

    def over_groups(value):
        step = chunk
        while step < rows:
            value = value + pltpu.roll(value, step, 1)
            step *= 2
        return value

    def tiles(n, body, unroll=2):
        def step(i, carry):
            body(pl.multiple_of(i * TILE, TILE))
            return carry

        lax.fori_loop(0, n // TILE, step, 0, unroll=unroll)

    send_tilt[...] = jnp.full(send_tilt.shape, tilts[0].astype(jnp.float32))
    for which, source in enumerate((phase, direction)):
        for f in range(frames):
            for base in range(0, sub, TILE):
                loaded = [
                    source[f, pl.ds(base * pieces + j, TILE, stride=pieces), :]
                    for j in range(pieces)
                ]
                for k in range(chunks):
                    send_lines[which, f * chunks + k, base : base + TILE] = at_lanes(
                        [turned(loaded[j], (j - k) * chunk) for j in range(pieces)]
                    )

    pl.semaphore_wait(barrier, len(peers))

    my_lines = pl.ds(pl.multiple_of(mod * sub, sub), sub)
    tilt_copies, line_copies = [], [[], []]
    for o in range(1, mod_count):
        tilt_copies.append(
            pltpu.make_async_remote_copy(
                send_tilt,
                tilt_tiles.at[mod],
                line_send.at[2, o - 1],
                line_recv.at[2, o - 1],
                device_id=peer(0, o),
                device_id_type=pl.DeviceIdType.MESH,
            )
        )
        for which in range(2):
            line_copies[which].append(
                pltpu.make_async_remote_copy(
                    send_lines.at[which, (mod + o) % mod_count],
                    lines.at[which, my_lines],
                    line_send.at[which, o - 1],
                    line_recv.at[which, o - 1],
                    device_id=peer(0, o),
                    device_id_type=pl.DeviceIdType.MESH,
                )
            )
    for copy in tilt_copies + line_copies[0]:
        copy.start()

    halos = []
    for da in (-1, 0, 1):
        for db in (-1, 0, 1):
            if (da, db) == (0, 0):
                continue
            src_f, dst_f, n_f = {1: (frames - 1, 0, 1), 0: (0, 1, frames), -1: (0, frames + 1, 1)}[da]
            src_x, dst_x, n_x = {
                1: (width - HALO, 0, HALO),
                0: (0, HALO, width),
                -1: (0, HALO + width, HALO),
            }[db]
            slot = len(halos)
            copy = pltpu.make_async_remote_copy(
                direction.at[pl.ds(src_f, n_f), pl.ds(src_x, n_x)],
                extended.at[pl.ds(dst_f, n_f), pl.ds(dst_x, n_x)],
                halo_send.at[slot],
                halo_recv.at[slot],
                device_id=peer(da, db),
                device_id_type=pl.DeviceIdType.MESH,
            )
            sends = (tm + da >= 0) & (tm + da < tm_count) & (mod + db >= 0) & (mod + db < mod_count)
            takes = (tm - da >= 0) & (tm - da < tm_count) & (mod - db >= 0) & (mod - db < mod_count)
            halos.append((copy, sends, takes, (dst_f, n_f, dst_x, n_x)))
            pl.when(sends)(copy.start)
    for copy in line_copies[1]:
        copy.start()

    for which in range(2):
        lines[which, my_lines] = send_lines[which, mod]
    tilt_tiles[mod] = send_tilt[...]
    extended[1 : 1 + frames, HALO : HALO + width] = direction[...]
    for _, _, takes, (dst_f, n_f, dst_x, n_x) in halos:

        @pl.when(jnp.logical_not(takes))
        def _():
            extended[dst_f : dst_f + n_f, dst_x : dst_x + n_x] = jnp.zeros(
                (n_f, n_x, rows), jnp.float32
            )

    copies[1].wait()
    copies[0].wait()

    def pack_own(source, base, row):
        return at_lanes(
            [
                pltpu.roll(
                    source[pl.ds(base + row * pieces + j, TILE, stride=pieces), :],
                    ((j + chunks - own_chunk) % chunks) * chunk,
                    1,
                )
                for j in range(pieces)
            ]
        )

    def pack_rows(row):
        packed_mask[pl.ds(row, TILE)] = pack_own(mask, 0, row).astype(jnp.float32)
        for side in range(2):
            packed_noise[side, pl.ds(row, TILE)] = pack_own(noise, side * pupil, row)

    tiles(packed_rows, pack_rows)

    for copy in tilt_copies:
        copy.wait_recv()

    def turn_rows(row):
        for l in range(groups):
            tilt = at_lanes([tilt_tiles[l * pieces + m] for m in range(pieces)]).astype(jnp.int32)
            tilt = jnp.concatenate([tilt] * (TILE // tilt.shape[0]), axis=0)
            index = row + lax.broadcasted_iota(jnp.int32, (TILE, rows), 0)
            for j in range(pieces):
                position = half + pieces * index + j
                product = tilt * position
                if length & (length - 1) == 0:
                    product = product & (length - 1)
                else:
                    product = product % length
                cosine, sine = cos_sin(
                    np.float32(2.0 * np.pi / length) * product.astype(jnp.float32)
                )
                turn[0, j, pl.ds(row, TILE), l * rows : (l + 1) * rows] = cosine
                turn[1, j, pl.ds(row, TILE), l * rows : (l + 1) * rows] = sine

    tiles(packed_rows, turn_rows)

    def place(j, row):
        return j % 2, pl.ds(pl.multiple_of((j // 2) * packed_rows + row, TILE), TILE)

    def put_operand(j, row, l, real, imag):
        for part, value in enumerate((real, imag)):
            parity, _ = place(j, row)
            high, low = split(value)
            columns = slice(part * lanes + l * rows, part * lanes + (l + 1) * rows)
            start = (j // 2) * packed_rows + row
            for copy_index, item in enumerate((high, low, high)):
                operand[parity, pl.ds(pl.multiple_of(copy_index * half + start, TILE), TILE), columns] = item

    def couple(target):
        for parity in range(2):
            target[1 - parity] = jnp.dot(
                table[parity], operand[parity], preferred_element_type=jnp.float32
            )

    def columns_of(part, l):
        return slice(part * lanes + l * rows, part * lanes + (l + 1) * rows)

    for copy in line_copies[0]:
        copy.wait_recv()

    def field_rows(row):
        cosine, sine = cos_sin(lines[0, pl.ds(row, TILE)])
        lit = packed_mask[pl.ds(row, TILE)]
        wide_cos, wide_sin = widened(cosine * lit), widened(sine * lit)
        for j in range(pieces):
            parity, where = place(j, row)
            for l in range(groups):
                turn_cos = turn[0, j, pl.ds(row, TILE), l * rows : (l + 1) * rows]
                turn_sin = turn[1, j, pl.ds(row, TILE), l * rows : (l + 1) * rows]
                real = wide_cos[j] * turn_cos - wide_sin[j] * turn_sin
                imag = wide_cos[j] * turn_sin + wide_sin[j] * turn_cos
                field[parity, where, columns_of(0, l)] = real
                field[parity, where, columns_of(1, l)] = imag
                put_operand(j, row, l, real, imag)

    tiles(packed_rows, field_rows)
    copies[3].wait()
    couple(image)

    copies[2].wait()
    for copy, _, takes, _ in halos:
        pl.when(takes)(copy.wait_recv)
    before = pl.ds(
        pl.multiple_of(((mod + mod_count - 1) % mod_count) * width + (width - HALO), HALO), HALO
    )
    codes = jnp.concatenate(
        [wind[before], wind[pl.ds(pl.multiple_of(mod * width, HALO), width)]], axis=0
    )
    tall = HALO + width
    frac_x = ((codes & 3).astype(jnp.float32) + 0.5) * 0.25
    frac_r = ((codes >> 2).astype(jnp.float32) + 0.5) * 0.25
    stay_stay = (1.0 - frac_x) * (1.0 - frac_r)
    ahead_stay = frac_x * (1.0 - frac_r)
    stay_ahead = (1.0 - frac_x) * frac_r
    ahead_ahead = frac_x * frac_r
    lane = lax.broadcasted_iota(jnp.int32, (tall, rows), 1)
    pixel = mod * width - HALO + lax.broadcasted_iota(jnp.int32, (tall, rows), 0)
    total_frames = frames * tm_count
    for i in range(frames + 1):
        base = extended[i, 0:tall]
        ahead = extended[i, 1 : tall + 1]
        crossing = stay_ahead * jnp.where(lane == rows - 1, 0.0, pltpu.roll(base, rows - 1, 1))
        crossing += ahead_ahead * jnp.where(lane == rows - 1, 0.0, pltpu.roll(ahead, rows - 1, 1))
        moved = stay_stay * base + ahead_stay * ahead + crossing
        flow_id = tm * frames - 1 + i
        valid = (pixel >= 0) & (flow_id >= 0) & (flow_id <= total_frames - 2)
        flow = jnp.where(valid, extended[i + 1, 0:tall] - moved, 0.0)
        if i >= 1:
            near[0] = ahead_stay * flow
            near[1] = ahead_ahead * flow
            behind = (stay_ahead * flow)[HALO:] + near[1, HALO - 1 : HALO - 1 + width]
            spread = (
                (stay_stay * flow)[HALO:]
                + near[0, HALO - 1 : HALO - 1 + width]
                + jnp.where(lane[HALO:] == 0, 0.0, pltpu.roll(behind, 1, 1))
            )
            prior[i - 1] = prior[i - 1] - spread
        if i < frames:
            prior[i] = flow[HALO:]

    for copy in line_copies[1]:
        copy.wait_recv()

    def dir_rows(row):
        wide = widened(lines[1, pl.ds(row, TILE)])
        for j in range(pieces):
            parity, where = place(j, row)
            dir_wide[parity, where] = wide[j]
            for l in range(groups):
                real = field[parity, where, columns_of(0, l)] * wide[j]
                imag = field[parity, where, columns_of(1, l)] * wide[j]
                put_operand(j, row, l, real, imag)

    tiles(packed_rows, dir_rows)
    couple(push)

    def signal_rows(row):
        wide_noise = [widened(packed_noise[side, pl.ds(row, TILE)]) for side in range(2)]
        for j in range(pieces):
            parity, where = place(j, row)
            step = dir_wide[parity, where]
            even = odd = None
            for l in range(groups):
                er = field[parity, where, columns_of(0, l)]
                ei = field[parity, where, columns_of(1, l)]
                ur = image[parity, where, columns_of(0, l)]
                ui = image[parity, where, columns_of(1, l)]
                vr = push[parity, where, columns_of(0, l)]
                vi = push[parity, where, columns_of(1, l)]
                even_l = ui * vr - ur * vi
                odd_l = (ur * er + ui * ei) * step - (er * vr + ei * vi)
                even = even_l if even is None else even + even_l
                odd = odd_l if odd is None else odd + odd_l
            even = 2.0 * over_groups(even)
            odd = over_groups(odd)
            front = wide_noise[0][j] * (even + odd)
            back = wide_noise[1][j] * (even - odd)
            both = front + back
            differ = 0.5 * (front - back)
            bent[parity, where] = differ
            for l in range(groups):
                er = field[parity, where, columns_of(0, l)]
                ei = field[parity, where, columns_of(1, l)]
                ur = image[parity, where, columns_of(0, l)]
                ui = image[parity, where, columns_of(1, l)]
                put_operand(j, row, l, differ * er - both * ui, differ * ei + both * ur)

    tiles(packed_rows, signal_rows)
    couple(push)

    parts_own = tm * mod_count + mod

    def grad_rows(i, total):
        row = pl.multiple_of(i * TILE, TILE)
        grad = []
        for j in range(pieces):
            parity, where = place(j, row)
            differ = bent[parity, where]
            acc = None
            for l in range(groups):
                er = field[parity, where, columns_of(0, l)]
                ei = field[parity, where, columns_of(1, l)]
                kr = differ * image[parity, where, columns_of(0, l)] + push[parity, where, columns_of(0, l)]
                ki = differ * image[parity, where, columns_of(1, l)] + push[parity, where, columns_of(1, l)]
                term = er * kr + ei * ki
                acc = term if acc is None else acc + term
            grad.append(2.0 * over_groups(acc))
        packed = at_lanes(grad)
        send_grad[pl.ds(row, TILE)] = packed
        return total + packed * lines[1, pl.ds(row, TILE)]

    total = lax.fori_loop(
        0, packed_rows // TILE, grad_rows, jnp.zeros((TILE, rows), jnp.float32), unroll=2
    )
    total = total[:HALO] + total[HALO:]
    for f in range(frames):
        for base in range(0, width, HALO):
            total = total + prior[f, base : base + HALO] * direction[f, base : base + HALO]
    parts[parts_own] = total

    grad_copies = []
    for o in range(1, mod_count):
        owner = (mod + o) % mod_count
        grad_copies.append(
            pltpu.make_async_remote_copy(
                send_grad.at[pl.ds(pl.multiple_of(owner * sub, sub), sub)],
                grads.at[mod],
                grad_send.at[o - 1],
                grad_recv.at[o - 1],
                device_id=peer(0, o),
                device_id_type=pl.DeviceIdType.MESH,
            )
        )
        grad_copies[-1].start()
    part_copies = []
    for slot, (a, b) in enumerate(peers):
        part_copies.append(
            pltpu.make_async_remote_copy(
                parts.at[parts_own],
                parts.at[parts_own],
                part_send.at[slot],
                part_recv.at[slot],
                device_id=peer(a, b),
                device_id_type=pl.DeviceIdType.MESH,
            )
        )
        part_copies[-1].start()
    grads[mod] = send_grad[my_lines]

    for copy in tilt_copies + line_copies[0] + line_copies[1]:
        copy.wait_send()
    for copy, sends, _, _ in halos:
        pl.when(sends)(copy.wait_send)
    for copy in grad_copies:
        copy.wait()

    for f in range(frames):
        for base in range(0, sub, TILE):
            arrived = [grads[f * chunks + k, base : base + TILE] for k in range(chunks)]
            for j in range(pieces):
                where = pl.ds(base * pieces + j, TILE, stride=pieces)
                grad = at_lanes([turned(arrived[k], (k - j) * chunk) for k in range(chunks)])
                out[f, where, :] = grad + prior[f, where, :]

    for copy in part_copies:
        copy.wait()
    whole = parts[0]
    for n in range(1, tm_count * mod_count):
        whole = whole + parts[n]
    entries = float(total_frames * pupil * rows)
    curvature[0] = jnp.sum(whole) / entries


def fused_device(phase, direction, pupil_mask, mod_tilts, wind_codes, noise_weight):
    frames, width, rows = phase.shape
    tm_count, mod_count = lax.axis_size("tm"), lax.axis_size("mod")
    pieces = mod_count // frames
    sub = width // pieces
    pupil = width * mod_count
    half = pupil // 2
    lanes = mod_count // pieces * rows
    packed_rows = pupil // pieces
    everyone = tm_count * mod_count
    vmem, smem, hbm = (
        pl.BlockSpec(memory_space=pltpu.VMEM),
        pl.BlockSpec(memory_space=pltpu.SMEM),
        pl.BlockSpec(memory_space=pl.ANY),
    )
    f32, bf16 = jnp.float32, jnp.bfloat16
    dma = pltpu.SemaphoreType.DMA
    return pl.pallas_call(
        functools.partial(fused_kernel, (tm_count, mod_count)),
        out_shape=(
            jax.ShapeDtypeStruct(phase.shape, f32),
            jax.ShapeDtypeStruct((1,), f32),
        ),
        in_specs=[vmem, vmem, smem, hbm, hbm, hbm, hbm],
        out_specs=(vmem, smem),
        scratch_shapes=[
            pltpu.VMEM((2, mod_count, sub, rows), f32),
            pltpu.VMEM((2, packed_rows, rows), f32),
            pltpu.VMEM((8, rows), f32),
            pltpu.VMEM((mod_count, 8, rows), f32),
            pltpu.VMEM((frames + 2, width + 2 * HALO, rows), f32),
            pltpu.VMEM(pupil_mask.shape, jnp.int32),
            pltpu.VMEM(wind_codes.shape, jnp.int32),
            pltpu.VMEM(noise_weight.shape[1:], f32),
            pltpu.VMEM((2, half, 3 * half), bf16),
            pltpu.VMEM((packed_rows, rows), f32),
            pltpu.VMEM((2, packed_rows, rows), f32),
            pltpu.VMEM((2, pieces, packed_rows, lanes), f32),
            pltpu.VMEM((2, half, 2 * lanes), f32),
            pltpu.VMEM((2, 3 * half, 2 * lanes), bf16),
            pltpu.VMEM((2, half, 2 * lanes), f32),
            pltpu.VMEM((2, half, 2 * lanes), f32),
            pltpu.VMEM((2, half, rows), f32),
            pltpu.VMEM((2, half, rows), f32),
            pltpu.VMEM((frames, width, rows), f32),
            pltpu.VMEM((2, width + HALO, rows), f32),
            pltpu.VMEM((packed_rows, rows), f32),
            pltpu.VMEM((mod_count, sub, rows), f32),
            pltpu.VMEM((everyone, 8, rows), f32),
            dma((4,)),
            dma((3, mod_count - 1)),
            dma((3, mod_count - 1)),
            dma((8,)),
            dma((8,)),
            dma((mod_count - 1,)),
            dma((mod_count - 1,)),
            dma((everyone - 1,)),
            dma((everyone - 1,)),
        ],
        compiler_params=pltpu.CompilerParams(collective_id=0, has_side_effects=True),
    )(
        phase,
        direction,
        mod_tilts,
        pupil_mask,
        wind_codes,
        noise_weight,
        jnp.asarray(coupling_tables(pupil, pieces)),
    )


def device_program(phase, direction, pupil_mask, mod_tilts, wind_codes, noise_weight):
    frames, width, rows = phase.shape
    mod_count = lax.axis_size("mod")
    fits = mod_count % frames == 0 and mod_tilts.shape[0] == 1 and frames > 1
    if fits:
        pieces = mod_count // frames
        fits = (
            pieces % 2 == 0
            and rows == 128
            and rows % pieces == 0
            and width % (pieces * TILE) == 0
            and pieces & (pieces - 1) == 0
        )
    run = fused_device if fits else per_device
    return run(phase, direction, pupil_mask, mod_tilts, wind_codes, noise_weight)


def solution(mesh):
    return jax.shard_map(
        device_program,
        mesh=mesh,
        in_specs=(
            P(("grp", "tm"), "mod", None),
            P(("grp", "tm"), "mod", None),
            P(),
            P("mod"),
            P("grp", None),
            P(("grp", "tm"), None, None),
        ),
        out_specs=(P(("grp", "tm"), "mod", None), P("grp")),
        check_vma=False,
    )
```

```python
import functools

import jax
import jax.numpy as jnp
import numpy as np
from jax import lax
from jax.experimental import pallas as pl
from jax.experimental.pallas import tpu as pltpu
from jax.sharding import PartitionSpec as P

HIGHEST = lax.Precision.HIGHEST


def with_halo(cells, sides, width):
    for axis, dim in sides:
        count = lax.axis_size(axis)
        ends = count - 1
        head = lax.slice_in_dim(cells, 0, width, axis=dim)
        tail = lax.slice_in_dim(cells, cells.shape[dim] - width, cells.shape[dim], axis=dim)
        cells = jnp.concatenate(
            [
                lax.ppermute(tail, axis, [(i, (i + 1) % count) for i in range(ends)]),
                cells,
                lax.ppermute(head, axis, [((i + 1) % count, i) for i in range(ends)]),
            ],
            axis=dim,
        )
    return cells


def square_table(count, orient):
    index_range = jnp.arange(count, dtype=jnp.int32)
    turn_counts = index_range[:, None] * index_range[None, :] % count
    angles = orient * 2.0 * jnp.pi / count * turn_counts.astype(jnp.float32)
    return (jnp.cos(angles), jnp.sin(angles))


def complex_mix(form, table_real, table_imag, field_real, field_imag):
    real_real = jnp.einsum(form, table_real, field_real, precision=HIGHEST)
    imag_imag = jnp.einsum(form, table_imag, field_imag, precision=HIGHEST)
    real_imag = jnp.einsum(form, table_real, field_imag, precision=HIGHEST)
    imag_real = jnp.einsum(form, table_imag, field_real, precision=HIGHEST)
    return (real_real - imag_imag, real_imag + imag_real)


def transform(field_real, field_imag, orient):
    batch_size, length, row_count = field_real.shape
    outer_size = 32
    inner_size = length // outer_size
    first_real, first_imag = square_table(outer_size, orient)
    second_real, second_imag = square_table(inner_size, orient)
    turn_counts = (
        jnp.arange(outer_size, dtype=jnp.int32)[:, None]
        * jnp.arange(inner_size, dtype=jnp.int32)[None, :]
        % length
    )
    angles = orient * 2.0 * jnp.pi / length * turn_counts.astype(jnp.float32)
    twist_real = jnp.cos(angles)[None, :, :, None]
    twist_imag = jnp.sin(angles)[None, :, :, None]
    shaped_real = field_real.reshape(batch_size, outer_size, inner_size, row_count)
    shaped_imag = field_imag.reshape(batch_size, outer_size, inner_size, row_count)
    section_real, section_imag = complex_mix(
        "kn,bnmr->bkmr", first_real, first_imag, shaped_real, shaped_imag
    )
    turned_real = section_real * twist_real - section_imag * twist_imag
    turned_imag = section_real * twist_imag + section_imag * twist_real
    final_real, final_imag = complex_mix(
        "dm,bkmr->bdkr", second_real, second_imag, turned_real, turned_imag
    )
    return (
        final_real.reshape(batch_size, length, row_count),
        final_imag.reshape(batch_size, length, row_count),
    )


def roof_mask(length, shift_bins):
    freq_index = jnp.arange(length, dtype=jnp.int32)
    signed_freq = jnp.where(freq_index < length // 2, freq_index, freq_index - length)
    turn_counts = shift_bins * jnp.abs(signed_freq) % length
    angles = -2.0 * jnp.pi / length * turn_counts.astype(jnp.float32)
    return (jnp.cos(angles), jnp.sin(angles))


def pyramid(field_real, field_imag, gain_real, gain_imag):
    spectrum_real, spectrum_imag = transform(field_real, field_imag, -1.0)
    column_real = gain_real[None, :, None]
    column_imag = gain_imag[None, :, None]
    masked_real = spectrum_real * column_real - spectrum_imag * column_imag
    masked_imag = spectrum_real * column_imag + spectrum_imag * column_real
    back_real, back_imag = transform(masked_real, masked_imag, 1.0)
    inverse_length = 1.0 / field_real.shape[1]
    return (back_real * inverse_length, back_imag * inverse_length)


def row_ahead(field):
    return jnp.pad(field[:, :, 1:], ((0, 0), (0, 0), (0, 1)))


def row_behind(field):
    return jnp.pad(field[:, :, :-1], ((0, 0), (0, 0), (1, 0)))


def flow_terms(extended, frac_x, frac_r, first_frame, total_frames, first_pixel):
    frames_ext, width_ext, row_count = extended.shape
    frames_dev = frames_ext - 2
    near_x = jnp.pad(frac_x, ((1, 0), (0, 0)))
    near_r = jnp.pad(frac_r, ((1, 0), (0, 0)))
    stay_stay = (1.0 - near_x) * (1.0 - near_r)
    ahead_stay = near_x * (1.0 - near_r)
    stay_ahead = (1.0 - near_x) * near_r
    ahead_ahead = near_x * near_r
    base_cells = extended[:, :-1, :]
    ahead_cells = extended[:, 1:, :]
    moved = (
        stay_stay * base_cells
        + ahead_stay * ahead_cells
        + stay_ahead * row_ahead(base_cells)
        + ahead_ahead * row_ahead(ahead_cells)
    )
    flow = extended[1:, :-1, :] - moved[:-1]
    frame_ids = first_frame - 1 + lax.broadcasted_iota(jnp.int32, flow.shape, 0)
    pixel_ids = first_pixel - 1 + lax.broadcasted_iota(jnp.int32, flow.shape, 1)
    valid = (frame_ids >= 0) & (frame_ids <= total_frames - 2) & (pixel_ids >= 0)
    flow = jnp.where(valid, flow, 0.0)
    spread = (
        (stay_stay * flow)[:, 1:]
        + (ahead_stay * flow)[:, :-1]
        + row_behind((stay_ahead * flow)[:, 1:] + (ahead_ahead * flow)[:, :-1])
    )
    prior = flow[:frames_dev, 1:] - spread[1:]
    return (prior, flow[1:, 1:])


def forward_pass(full_phase, full_direction, tilts, amplitude, gain_real, gain_imag):
    frames_dev, pupil_width, row_count = full_phase.shape
    line_length = 2 * pupil_width
    quarter = pupil_width // 2
    local_points = tilts.shape[0]
    positions = quarter + jnp.arange(pupil_width, dtype=jnp.int32)
    tilt_turns = tilts[:, None] * positions[None, :] % line_length
    tilt_angles = 2.0 * jnp.pi / line_length * tilt_turns.astype(jnp.float32)
    angles = full_phase[None] + tilt_angles[:, None, :, None]
    field_real = amplitude * jnp.cos(angles)
    field_imag = amplitude * jnp.sin(angles)
    margins = ((0, 0), (quarter, quarter), (0, 0))
    line_batch = local_points * frames_dev

    def padded_lines(field):
        return jnp.pad(field.reshape(line_batch, pupil_width, row_count), margins)

    image_real, image_imag = pyramid(
        padded_lines(field_real), padded_lines(field_imag), gain_real, gain_imag
    )
    push_real, push_imag = pyramid(
        padded_lines(-field_imag * full_direction),
        padded_lines(field_real * full_direction),
        gain_real,
        gain_imag,
    )
    signal_terms = (2.0 * (image_real * push_real + image_imag * push_imag)).reshape(
        local_points, frames_dev, line_length, row_count
    )
    return (field_real, field_imag, image_real, image_imag, jnp.sum(signal_terms, axis=0))


def backward_pass(
    field_real, field_imag, image_real, image_imag, weighted_full, gain_real, gain_imag
):
    local_points, frames_dev, pupil_width, row_count = field_real.shape
    line_length = 2 * pupil_width
    quarter = pupil_width // 2
    line_batch = local_points * frames_dev
    image_shaped_real = image_real.reshape(local_points, frames_dev, line_length, row_count)
    image_shaped_imag = image_imag.reshape(local_points, frames_dev, line_length, row_count)
    source_real = (weighted_full[None] * image_shaped_real).reshape(
        line_batch, line_length, row_count
    )
    source_imag = (weighted_full[None] * image_shaped_imag).reshape(
        line_batch, line_length, row_count
    )
    back_real, back_imag = pyramid(source_real, source_imag, gain_real, -gain_imag)
    back_real = back_real[:, quarter : quarter + pupil_width].reshape(
        local_points, frames_dev, pupil_width, row_count
    )
    back_imag = back_imag[:, quarter : quarter + pupil_width].reshape(
        local_points, frames_dev, pupil_width, row_count
    )
    return -2.0 * jnp.sum(field_imag * back_real - field_real * back_imag, axis=0)


def per_device(phase, direction, pupil_mask, mod_tilts, wind_codes, noise_weight):
    frames_dev, shard_width, row_count = phase.shape
    mod_count = lax.axis_size("mod")
    pupil_width = shard_width * mod_count
    line_length = 2 * pupil_width
    quarter = pupil_width // 2
    mod_index = lax.axis_index("mod")
    first_frame = lax.axis_index("tm") * frames_dev
    total_frames = frames_dev * lax.axis_size("tm")
    first_pixel = mod_index * shard_width
    frac_x = ((wind_codes % 4).astype(jnp.float32) + 0.5) / 4.0
    frac_r = ((wind_codes // 4).astype(jnp.float32) + 0.5) / 4.0
    gain_real, gain_imag = roof_mask(line_length, quarter)
    rimmed = with_halo(direction, (("tm", 0),), 1)
    full_phase, full_rim = (
        lax.all_gather(phase, "mod", axis=1, tiled=True),
        lax.all_gather(rimmed, "mod", axis=1, tiled=True),
    )
    full_direction = full_rim[1:-1]
    extended = jnp.pad(full_rim, ((0, 0), (1, 1), (0, 0)))
    prior_lines, flow_lines = flow_terms(extended, frac_x, frac_r, first_frame, total_frames, 0)
    prior = lax.dynamic_slice_in_dim(prior_lines, first_pixel, shard_width, 1)
    amplitude = pupil_mask.astype(jnp.float32)
    field_real, field_imag, image_real, image_imag, signal_local = forward_pass(
        full_phase, full_direction, mod_tilts, amplitude, gain_real, gain_imag
    )
    signal_full = lax.psum(signal_local, "mod")
    weighted_used = noise_weight * signal_full
    grad_lines = backward_pass(
        field_real, field_imag, image_real, image_imag, weighted_used, gain_real, gain_imag
    )
    grad_own = lax.psum_scatter(grad_lines, "mod", scatter_dimension=1, tiled=True)
    hess_vec = grad_own + prior
    curvature_total = lax.psum(jnp.sum(direction * hess_vec), ("tm", "mod"))
    entry_count = float(total_frames * pupil_width * row_count)
    curvature = (curvature_total / entry_count).reshape(1)
    return (hess_vec, curvature)


TILE = 16
HALO = 8


def coupling_tables(pupil_width, pieces):
    per_piece = pupil_width // pieces
    order = [
        np.concatenate([pieces * np.arange(per_piece) + j for j in range(parity, pieces, 2)])
        for parity in (0, 1)
    ]
    tables = []
    for source in (0, 1):
        gap = order[1 - source][:, None] - order[source][None, :]
        exact = -1.0 / (pupil_width * np.sin(np.pi * gap / pupil_width))
        high = exact.astype(jnp.bfloat16)
        low = (exact - high.astype(np.float64)).astype(jnp.bfloat16)
        tables.append(np.concatenate([high, high, low], axis=1))
    return np.stack(tables)


def cos_sin(angle):
    turns = jnp.round(angle * np.float32(2.0 / np.pi))
    rest = angle - turns * np.float32(1.5703125)
    rest = rest - turns * np.float32(4.837512969970703125e-4)
    rest = rest - turns * np.float32(7.54978995489188216e-8)
    square = rest * rest
    sine = rest + rest * square * (
        np.float32(-1.6666654611e-1)
        + square * (np.float32(8.3321608736e-3) + square * np.float32(-1.9515295891e-4))
    )
    cosine = (
        1.0
        - 0.5 * square
        + square
        * square
        * (
            np.float32(4.166664568298827e-2)
            + square * (np.float32(-1.388731625493765e-3) + square * np.float32(2.443315711809948e-5))
        )
    )
    quarter = turns.astype(jnp.int32)
    swap = (quarter & 1) == 1
    out_cos = jnp.where(swap, sine, cosine)
    out_sin = jnp.where(swap, cosine, sine)
    out_cos = jnp.where(((quarter + 1) & 2) == 2, -out_cos, out_cos)
    out_sin = jnp.where((quarter & 2) == 2, -out_sin, out_sin)
    return out_cos, out_sin


def split(value):
    high = value.astype(jnp.bfloat16)
    return high, (value - high.astype(jnp.float32)).astype(jnp.bfloat16)


def fused_kernel(
    counts,
    phase,
    direction,
    tilts_hbm,
    mask_hbm,
    wind_hbm,
    noise_hbm,
    table_hbm,
    grads,
    prior,
    parts,
    send_lines,
    lines,
    send_tilt,
    tilt_tiles,
    extended,
    mask,
    wind,
    noise,
    table,
    packed_mask,
    packed_noise,
    turn,
    field,
    operand,
    image,
    push,
    dir_wide,
    bent,
    near,
    send_grad,
    tilts,
    local_sem,
    line_send,
    line_recv,
    halo_send,
    halo_recv,
    grad_send,
    grad_recv,
    part_send,
    part_recv,
    entered,
):
    tm_count, mod_count = counts
    frames, width, rows = phase.shape
    chunks = mod_count // frames
    chunk = rows // chunks
    pieces = chunks
    sub = width // pieces
    pupil = width * mod_count
    length = 2 * pupil
    packed_rows = pupil // pieces
    half = pupil // 2
    groups = mod_count // pieces
    lanes = groups * rows
    tm = lax.axis_index("tm")
    mod = lax.axis_index("mod")
    own_frame = mod // chunks
    own_chunk = mod % chunks

    copies = [
        pltpu.make_async_copy(noise_hbm.at[own_frame], noise, local_sem.at[0]),
        pltpu.make_async_copy(mask_hbm, mask, local_sem.at[1]),
        pltpu.make_async_copy(wind_hbm, wind, local_sem.at[2]),
        pltpu.make_async_copy(table_hbm, table, local_sem.at[3]),
        pltpu.make_async_copy(tilts_hbm, tilts, local_sem.at[4]),
    ]

    barrier = pltpu.get_barrier_semaphore()
    peers = [
        (a, b) for a in range(tm_count) for b in range(mod_count) if (a, b) != (0, 0)
    ]

    def peer(a, b):
        return {"tm": (tm + a) % tm_count, "mod": (mod + b) % mod_count}

    for b in range(1, mod_count):
        pl.semaphore_signal(
            barrier, inc=1, device_id=peer(0, b), device_id_type=pl.DeviceIdType.MESH
        )
    beside = [(-1, tm > 0), (1, tm < tm_count - 1)]

    def tell_beside(semaphores):
        for side, (step, exists) in enumerate(beside):

            @pl.when(exists)
            def _():
                pl.semaphore_signal(
                    semaphores[1 - side],
                    inc=1,
                    device_id=peer(step, 0),
                    device_id_type=pl.DeviceIdType.MESH,
                )

    def hear_beside(semaphores):
        for side, (step, exists) in enumerate(beside):

            @pl.when(exists)
            def _():
                pl.semaphore_wait(semaphores[side], 1)

    def entered_at(n):
        return [entered.at[n, 0], entered.at[n, 1]]

    tell_beside([barrier, barrier])
    for copy in copies:
        copy.start()

    lane_group = lax.broadcasted_iota(jnp.int32, (TILE, rows), 1) // chunk

    def at_lanes(values):
        out_value = values[0]
        for j in range(1, len(values)):
            out_value = jnp.where(lane_group[: out_value.shape[0]] == j, values[j], out_value)
        return out_value

    def turned(value, amount):
        if isinstance(amount, int):
            amount = amount % rows
            if amount == 0:
                return value
        return pltpu.roll(value, amount, 1)

    def widened(value):
        shifts = [turned(value, s * chunk) for s in range(pieces)]
        return [
            at_lanes([shifts[(m - j) % pieces] for m in range(pieces)]) for j in range(pieces)
        ]

    def over_groups(value):
        step = chunk
        while step < rows:
            value = value + pltpu.roll(value, step, 1)
            step *= 2
        return value

    def tiles(n, body, unroll=2):
        def step(i, carry):
            body(pl.multiple_of(i * TILE, TILE))
            return carry

        lax.fori_loop(0, n // TILE, step, 0, unroll=unroll)

    for which, source in enumerate((phase, direction)):
        for f in range(frames):
            for base in range(0, sub, TILE):
                loaded = [
                    source[f, pl.ds(base * pieces + j, TILE, stride=pieces), :]
                    for j in range(pieces)
                ]
                for k in range(chunks):
                    send_lines[which, f * chunks + k, base : base + TILE] = at_lanes(
                        [turned(loaded[j], (j - k) * chunk) for j in range(pieces)]
                    )

    copies[4].wait()
    send_tilt[...] = jnp.full(send_tilt.shape, tilts[0].astype(jnp.float32))
    earlier, later = (tm + tm_count - 1) // tm_count, (2 * tm_count - 2 - tm) // tm_count
    pl.semaphore_wait(barrier, mod_count - 1 + earlier + later)

    my_lines = pl.ds(pl.multiple_of(mod * sub, sub), sub)
    tilt_copies, line_copies = [], [[], []]
    for o in range(1, mod_count):
        tilt_copies.append(
            pltpu.make_async_remote_copy(
                send_tilt,
                tilt_tiles.at[mod],
                line_send.at[2, o - 1],
                line_recv.at[2, o - 1],
                device_id=peer(0, o),
                device_id_type=pl.DeviceIdType.MESH,
            )
        )
        for which in range(2):
            line_copies[which].append(
                pltpu.make_async_remote_copy(
                    send_lines.at[which, (mod + o) % mod_count],
                    lines.at[which, my_lines],
                    line_send.at[which, o - 1],
                    line_recv.at[which, o - 1],
                    device_id=peer(0, o),
                    device_id_type=pl.DeviceIdType.MESH,
                )
            )
    for copy in tilt_copies + line_copies[0]:
        copy.start()
    tell_beside(entered_at(0))

    halos, corners = [], []
    for da in (-1, 0, 1):
        for db in (-1, 0, 1):
            if (da, db) == (0, 0):
                continue
            src_f, dst_f, n_f = {1: (frames - 1, 0, 1), 0: (0, 1, frames), -1: (0, frames + 1, 1)}[da]
            src_x, dst_x, n_x = {
                1: (width - HALO, 0, HALO),
                0: (0, HALO, width),
                -1: (0, HALO + width, HALO),
            }[db]
            slot = len(halos)
            copy = pltpu.make_async_remote_copy(
                direction.at[pl.ds(src_f, n_f), pl.ds(src_x, n_x)],
                extended.at[pl.ds(dst_f, n_f), pl.ds(dst_x, n_x)],
                halo_send.at[slot],
                halo_recv.at[slot],
                device_id=peer(da, db),
                device_id_type=pl.DeviceIdType.MESH,
            )
            sends = (tm + da >= 0) & (tm + da < tm_count) & (mod + db >= 0) & (mod + db < mod_count)
            takes = (tm - da >= 0) & (tm - da < tm_count) & (mod - db >= 0) & (mod - db < mod_count)
            halos.append((copy, sends, takes, (dst_f, n_f, dst_x, n_x)))
            if da == 0 or db == 0:
                pl.when(sends)(copy.start)
            else:
                corners.append((copy, sends))
    for copy in line_copies[1]:
        copy.start()

    for which in range(2):
        lines[which, my_lines] = send_lines[which, mod]
    tilt_tiles[mod] = send_tilt[...]
    extended[1 : 1 + frames, HALO : HALO + width] = direction[...]
    for _, _, takes, (dst_f, n_f, dst_x, n_x) in halos:

        @pl.when(jnp.logical_not(takes))
        def _():
            extended[dst_f : dst_f + n_f, dst_x : dst_x + n_x] = jnp.zeros(
                (n_f, n_x, rows), jnp.float32
            )

    copies[1].wait()
    copies[0].wait()

    def pack_own(source, base, row):
        return at_lanes(
            [
                pltpu.roll(
                    source[pl.ds(base + row * pieces + j, TILE, stride=pieces), :],
                    ((j + chunks - own_chunk) % chunks) * chunk,
                    1,
                )
                for j in range(pieces)
            ]
        )

    def pack_rows(row):
        packed_mask[pl.ds(row, TILE)] = pack_own(mask, 0, row).astype(jnp.float32)
        for side in range(2):
            packed_noise[side, pl.ds(row, TILE)] = pack_own(noise, side * pupil, row)

    tiles(packed_rows, pack_rows)

    hear_beside(entered_at(0))
    for copy, sends in corners:
        pl.when(sends)(copy.start)
    if tm_count > 2:
        tell_beside(entered_at(1))
    for copy in tilt_copies:
        copy.wait_recv()

    def turn_rows(row):
        for l in range(groups):
            tilt = at_lanes([tilt_tiles[l * pieces + m] for m in range(pieces)]).astype(jnp.int32)
            tilt = jnp.concatenate([tilt] * (TILE // tilt.shape[0]), axis=0)
            index = row + lax.broadcasted_iota(jnp.int32, (TILE, rows), 0)
            for j in range(pieces):
                position = half + pieces * index + j
                product = tilt * position
                if length & (length - 1) == 0:
                    product = product & (length - 1)
                else:
                    product = product % length
                cosine, sine = cos_sin(
                    np.float32(2.0 * np.pi / length) * product.astype(jnp.float32)
                )
                turn[0, j, pl.ds(row, TILE), l * rows : (l + 1) * rows] = cosine
                turn[1, j, pl.ds(row, TILE), l * rows : (l + 1) * rows] = sine

    tiles(packed_rows, turn_rows)

    def place(j, row):
        return j % 2, pl.ds(pl.multiple_of((j // 2) * packed_rows + row, TILE), TILE)

    def put_operand(j, row, l, real, imag):
        for part, value in enumerate((real, imag)):
            parity, _ = place(j, row)
            high, low = split(value)
            columns = slice(part * lanes + l * rows, part * lanes + (l + 1) * rows)
            start = (j // 2) * packed_rows + row
            for copy_index, item in enumerate((high, low, high)):
                operand[parity, pl.ds(pl.multiple_of(copy_index * half + start, TILE), TILE), columns] = item

    def couple(target):
        for parity in range(2):
            target[1 - parity] = jnp.dot(
                table[parity], operand[parity], preferred_element_type=jnp.float32
            )

    def columns_of(part, l):
        return slice(part * lanes + l * rows, part * lanes + (l + 1) * rows)

    for n in range(1, tm_count - 1):
        hear_beside(entered_at(n))
        if n < tm_count - 2:
            tell_beside(entered_at(n + 1))
    for copy in line_copies[0]:
        copy.wait_recv()

    def field_rows(row):
        cosine, sine = cos_sin(lines[0, pl.ds(row, TILE)])
        lit = packed_mask[pl.ds(row, TILE)]
        wide_cos, wide_sin = widened(cosine * lit), widened(sine * lit)
        for j in range(pieces):
            parity, where = place(j, row)
            for l in range(groups):
                turn_cos = turn[0, j, pl.ds(row, TILE), l * rows : (l + 1) * rows]
                turn_sin = turn[1, j, pl.ds(row, TILE), l * rows : (l + 1) * rows]
                real = wide_cos[j] * turn_cos - wide_sin[j] * turn_sin
                imag = wide_cos[j] * turn_sin + wide_sin[j] * turn_cos
                field[parity, where, columns_of(0, l)] = real
                field[parity, where, columns_of(1, l)] = imag
                put_operand(j, row, l, real, imag)

    tiles(packed_rows, field_rows)
    copies[3].wait()
    couple(image)

    copies[2].wait()
    for copy, _, takes, _ in halos:
        pl.when(takes)(copy.wait_recv)
    before = pl.ds(
        pl.multiple_of(((mod + mod_count - 1) % mod_count) * width + (width - HALO), HALO), HALO
    )
    codes = jnp.concatenate(
        [wind[before], wind[pl.ds(pl.multiple_of(mod * width, HALO), width)]], axis=0
    )
    tall = HALO + width
    frac_x = ((codes & 3).astype(jnp.float32) + 0.5) * 0.25
    frac_r = ((codes >> 2).astype(jnp.float32) + 0.5) * 0.25
    stay_stay = (1.0 - frac_x) * (1.0 - frac_r)
    ahead_stay = frac_x * (1.0 - frac_r)
    stay_ahead = (1.0 - frac_x) * frac_r
    ahead_ahead = frac_x * frac_r
    lane = lax.broadcasted_iota(jnp.int32, (tall, rows), 1)
    pixel = mod * width - HALO + lax.broadcasted_iota(jnp.int32, (tall, rows), 0)
    total_frames = frames * tm_count
    flow_power = jnp.zeros((HALO, rows), jnp.float32)
    for i in range(frames + 1):
        base = extended[i, 0:tall]
        ahead = extended[i, 1 : tall + 1]
        crossing = stay_ahead * jnp.where(lane == rows - 1, 0.0, pltpu.roll(base, rows - 1, 1))
        crossing += ahead_ahead * jnp.where(lane == rows - 1, 0.0, pltpu.roll(ahead, rows - 1, 1))
        moved = stay_stay * base + ahead_stay * ahead + crossing
        flow_id = tm * frames - 1 + i
        valid = (pixel >= 0) & (flow_id >= 0) & (flow_id <= total_frames - 2)
        flow = jnp.where(valid, extended[i + 1, 0:tall] - moved, 0.0)
        if i >= 1:
            for start in range(HALO, tall, HALO):
                flow_power += flow[start : start + HALO] * flow[start : start + HALO]
            near[0] = ahead_stay * flow
            near[1] = ahead_ahead * flow
            behind = (stay_ahead * flow)[HALO:] + near[1, HALO - 1 : HALO - 1 + width]
            spread = (
                (stay_stay * flow)[HALO:]
                + near[0, HALO - 1 : HALO - 1 + width]
                + jnp.where(lane[HALO:] == 0, 0.0, pltpu.roll(behind, 1, 1))
            )
            prior[i - 1] = prior[i - 1] - spread
        if i < frames:
            prior[i] = flow[HALO:]

    for copy in line_copies[1]:
        copy.wait_recv()

    def dir_rows(row):
        wide = widened(lines[1, pl.ds(row, TILE)])
        for j in range(pieces):
            parity, where = place(j, row)
            dir_wide[parity, where] = wide[j]
            for l in range(groups):
                real = field[parity, where, columns_of(0, l)] * wide[j]
                imag = field[parity, where, columns_of(1, l)] * wide[j]
                put_operand(j, row, l, real, imag)

    tiles(packed_rows, dir_rows)
    couple(push)

    def signal_rows(i, power):
        row = pl.multiple_of(i * TILE, TILE)
        wide_noise = [widened(packed_noise[side, pl.ds(row, TILE)]) for side in range(2)]
        for j in range(pieces):
            parity, where = place(j, row)
            step = dir_wide[parity, where]
            even = odd = None
            for l in range(groups):
                er = field[parity, where, columns_of(0, l)]
                ei = field[parity, where, columns_of(1, l)]
                ur = image[parity, where, columns_of(0, l)]
                ui = image[parity, where, columns_of(1, l)]
                vr = push[parity, where, columns_of(0, l)]
                vi = push[parity, where, columns_of(1, l)]
                even_l = ui * vr - ur * vi
                odd_l = (ur * er + ui * ei) * step - (er * vr + ei * vi)
                even = even_l if even is None else even + even_l
                odd = odd_l if odd is None else odd + odd_l
            even = 2.0 * over_groups(even)
            odd = over_groups(odd)
            front = wide_noise[0][j] * (even + odd)
            back = wide_noise[1][j] * (even - odd)
            power = power + front * (even + odd) + back * (even - odd)
            both = front + back
            differ = 0.5 * (front - back)
            bent[parity, where] = differ
            for l in range(groups):
                er = field[parity, where, columns_of(0, l)]
                ei = field[parity, where, columns_of(1, l)]
                ur = image[parity, where, columns_of(0, l)]
                ui = image[parity, where, columns_of(1, l)]
                put_operand(j, row, l, differ * er - both * ui, differ * ei + both * ur)

        return power

    power = lax.fori_loop(
        0, packed_rows // TILE, signal_rows, jnp.zeros((TILE, rows), jnp.float32), unroll=2
    )
    parts_own = tm * mod_count + mod
    parts[parts_own] = (power[:HALO] + power[HALO:]) * (1.0 / pieces) + flow_power
    part_copies = []
    for slot, (a, b) in enumerate(peers):
        part_copies.append(
            pltpu.make_async_remote_copy(
                parts.at[parts_own],
                parts.at[parts_own],
                part_send.at[slot],
                part_recv.at[slot],
                device_id=peer(a, b),
                device_id_type=pl.DeviceIdType.MESH,
            )
        )
        part_copies[-1].start()
    couple(push)

    def grad_rows(row):
        grad = []
        for j in range(pieces):
            parity, where = place(j, row)
            differ = bent[parity, where]
            acc = None
            for l in range(groups):
                er = field[parity, where, columns_of(0, l)]
                ei = field[parity, where, columns_of(1, l)]
                kr = differ * image[parity, where, columns_of(0, l)] + push[parity, where, columns_of(0, l)]
                ki = differ * image[parity, where, columns_of(1, l)] + push[parity, where, columns_of(1, l)]
                term = er * kr + ei * ki
                acc = term if acc is None else acc + term
            grad.append(2.0 * over_groups(acc))
        send_grad[pl.ds(row, TILE)] = at_lanes(grad)

    tiles(packed_rows, grad_rows)

    grad_copies = []
    for o in range(1, mod_count):
        owner = (mod + o) % mod_count
        grad_copies.append(
            pltpu.make_async_remote_copy(
                send_grad.at[pl.ds(pl.multiple_of(owner * sub, sub), sub)],
                grads.at[mod],
                grad_send.at[o - 1],
                grad_recv.at[o - 1],
                device_id=peer(0, o),
                device_id_type=pl.DeviceIdType.MESH,
            )
        )
        grad_copies[-1].start()
    grads[mod] = send_grad[my_lines]

    for copy in tilt_copies + line_copies[0] + line_copies[1]:
        copy.wait_send()
    for copy, sends, _, _ in halos:
        pl.when(sends)(copy.wait_send)
    for copy in grad_copies + part_copies:
        copy.wait()


def gather_kernel(entries, grads, prior, parts, out, curvature):
    frames, width, rows = prior.shape
    mod_count, sub, _ = grads.shape
    pieces = mod_count // frames
    chunk = rows // pieces
    lane_group = lax.broadcasted_iota(jnp.int32, (TILE, rows), 1) // chunk
    for f in range(frames):
        for base in range(0, sub, TILE):
            arrived = [grads[f * pieces + k, base : base + TILE] for k in range(pieces)]
            for j in range(pieces):
                where = pl.ds(base * pieces + j, TILE, stride=pieces)
                grad = None
                for k in range(pieces):
                    shift = (k - j) * chunk % rows
                    piece = pltpu.roll(arrived[k], shift, 1) if shift else arrived[k]
                    grad = piece if grad is None else jnp.where(lane_group == k, piece, grad)
                out[f, where, :] = grad + prior[f, where, :]
    whole = parts[0]
    for n in range(1, parts.shape[0]):
        whole = whole + parts[n]
    curvature[0] = jnp.sum(whole) / entries


def fused_device(phase, direction, pupil_mask, mod_tilts, wind_codes, noise_weight):
    frames, width, rows = phase.shape
    tm_count, mod_count = lax.axis_size("tm"), lax.axis_size("mod")
    pieces = mod_count // frames
    sub = width // pieces
    pupil = width * mod_count
    half = pupil // 2
    lanes = mod_count // pieces * rows
    packed_rows = pupil // pieces
    everyone = tm_count * mod_count
    vmem, smem, hbm = (
        pl.BlockSpec(memory_space=pltpu.VMEM),
        pl.BlockSpec(memory_space=pltpu.SMEM),
        pl.BlockSpec(memory_space=pl.ANY),
    )
    fixed = pl.BlockSpec(memory_space=pltpu.HBM)
    f32, bf16 = jnp.float32, jnp.bfloat16
    dma = pltpu.SemaphoreType.DMA
    sums = pl.pallas_call(
        functools.partial(fused_kernel, (tm_count, mod_count)),
        out_shape=(
            pltpu.VMEM((mod_count, sub, rows), f32),
            pltpu.VMEM(phase.shape, f32),
            pltpu.VMEM((everyone, HALO, rows), f32),
        ),
        in_specs=[vmem, vmem, fixed, hbm, hbm, hbm, hbm],
        out_specs=(vmem, vmem, vmem),
        scratch_shapes=[
            pltpu.VMEM((2, mod_count, sub, rows), f32),
            pltpu.VMEM((2, packed_rows, rows), f32),
            pltpu.VMEM((8, rows), f32),
            pltpu.VMEM((mod_count, 8, rows), f32),
            pltpu.VMEM((frames + 2, width + 2 * HALO, rows), f32),
            pltpu.VMEM(pupil_mask.shape, jnp.int32),
            pltpu.VMEM(wind_codes.shape, jnp.int32),
            pltpu.VMEM(noise_weight.shape[1:], f32),
            pltpu.VMEM((2, half, 3 * half), bf16),
            pltpu.VMEM((packed_rows, rows), f32),
            pltpu.VMEM((2, packed_rows, rows), f32),
            pltpu.VMEM((2, pieces, packed_rows, lanes), f32),
            pltpu.VMEM((2, half, 2 * lanes), f32),
            pltpu.VMEM((2, 3 * half, 2 * lanes), bf16),
            pltpu.VMEM((2, half, 2 * lanes), f32),
            pltpu.VMEM((2, half, 2 * lanes), f32),
            pltpu.VMEM((2, half, rows), f32),
            pltpu.VMEM((2, half, rows), f32),
            pltpu.VMEM((2, width + HALO, rows), f32),
            pltpu.VMEM((packed_rows, rows), f32),
            pltpu.SMEM((1,), jnp.int32),
            dma((5,)),
            dma((3, mod_count - 1)),
            dma((3, mod_count - 1)),
            dma((8,)),
            dma((8,)),
            dma((mod_count - 1,)),
            dma((mod_count - 1,)),
            dma((everyone - 1,)),
            dma((everyone - 1,)),
            pltpu.SemaphoreType.REGULAR((max(tm_count - 1, 1), 2)),
        ],
        compiler_params=pltpu.CompilerParams(collective_id=0, has_side_effects=True),
    )(
        phase,
        direction,
        mod_tilts,
        pupil_mask,
        wind_codes,
        noise_weight,
        jnp.asarray(coupling_tables(pupil, pieces)),
    )
    return pl.pallas_call(
        functools.partial(gather_kernel, float(frames * tm_count * pupil * rows)),
        out_shape=(jax.ShapeDtypeStruct(phase.shape, f32), jax.ShapeDtypeStruct((1,), f32)),
        in_specs=[vmem, vmem, vmem],
        out_specs=(vmem, smem),
    )(*[pltpu.with_memory_space_constraint(item, pltpu.VMEM) for item in sums])


def device_program(phase, direction, pupil_mask, mod_tilts, wind_codes, noise_weight):
    frames, width, rows = phase.shape
    mod_count = lax.axis_size("mod")
    fits = mod_count % frames == 0 and mod_tilts.shape[0] == 1 and frames > 1
    if fits:
        pieces = mod_count // frames
        fits = (
            lax.axis_size("tm") > 1
            and pieces % 2 == 0
            and rows == 128
            and rows % pieces == 0
            and width % (pieces * TILE) == 0
            and pieces & (pieces - 1) == 0
        )
    run = fused_device if fits else per_device
    return run(phase, direction, pupil_mask, mod_tilts, wind_codes, noise_weight)


def solution(mesh):
    return jax.shard_map(
        device_program,
        mesh=mesh,
        in_specs=(
            P(("grp", "tm"), "mod", None),
            P(("grp", "tm"), "mod", None),
            P(),
            P("mod"),
            P("grp", None),
            P(("grp", "tm"), None, None),
        ),
        out_specs=(P(("grp", "tm"), "mod", None), P("grp")),
        check_vma=False,
    )
```

```python
import functools

import jax
import jax.numpy as jnp
import numpy as np
from jax import lax
from jax.experimental import pallas as pl
from jax.experimental.pallas import tpu as pltpu
from jax.sharding import PartitionSpec as P

HIGHEST = lax.Precision.HIGHEST


def with_halo(cells, sides, width):
    for axis, dim in sides:
        count = lax.axis_size(axis)
        ends = count - 1
        head = lax.slice_in_dim(cells, 0, width, axis=dim)
        tail = lax.slice_in_dim(cells, cells.shape[dim] - width, cells.shape[dim], axis=dim)
        cells = jnp.concatenate(
            [
                lax.ppermute(tail, axis, [(i, (i + 1) % count) for i in range(ends)]),
                cells,
                lax.ppermute(head, axis, [((i + 1) % count, i) for i in range(ends)]),
            ],
            axis=dim,
        )
    return cells


def square_table(count, orient):
    index_range = jnp.arange(count, dtype=jnp.int32)
    turn_counts = index_range[:, None] * index_range[None, :] % count
    angles = orient * 2.0 * jnp.pi / count * turn_counts.astype(jnp.float32)
    return (jnp.cos(angles), jnp.sin(angles))


def complex_mix(form, table_real, table_imag, field_real, field_imag):
    real_real = jnp.einsum(form, table_real, field_real, precision=HIGHEST)
    imag_imag = jnp.einsum(form, table_imag, field_imag, precision=HIGHEST)
    real_imag = jnp.einsum(form, table_real, field_imag, precision=HIGHEST)
    imag_real = jnp.einsum(form, table_imag, field_real, precision=HIGHEST)
    return (real_real - imag_imag, real_imag + imag_real)


def transform(field_real, field_imag, orient):
    batch_size, length, row_count = field_real.shape
    outer_size = 32
    inner_size = length // outer_size
    first_real, first_imag = square_table(outer_size, orient)
    second_real, second_imag = square_table(inner_size, orient)
    turn_counts = (
        jnp.arange(outer_size, dtype=jnp.int32)[:, None]
        * jnp.arange(inner_size, dtype=jnp.int32)[None, :]
        % length
    )
    angles = orient * 2.0 * jnp.pi / length * turn_counts.astype(jnp.float32)
    twist_real = jnp.cos(angles)[None, :, :, None]
    twist_imag = jnp.sin(angles)[None, :, :, None]
    shaped_real = field_real.reshape(batch_size, outer_size, inner_size, row_count)
    shaped_imag = field_imag.reshape(batch_size, outer_size, inner_size, row_count)
    section_real, section_imag = complex_mix(
        "kn,bnmr->bkmr", first_real, first_imag, shaped_real, shaped_imag
    )
    turned_real = section_real * twist_real - section_imag * twist_imag
    turned_imag = section_real * twist_imag + section_imag * twist_real
    final_real, final_imag = complex_mix(
        "dm,bkmr->bdkr", second_real, second_imag, turned_real, turned_imag
    )
    return (
        final_real.reshape(batch_size, length, row_count),
        final_imag.reshape(batch_size, length, row_count),
    )


def roof_mask(length, shift_bins):
    freq_index = jnp.arange(length, dtype=jnp.int32)
    signed_freq = jnp.where(freq_index < length // 2, freq_index, freq_index - length)
    turn_counts = shift_bins * jnp.abs(signed_freq) % length
    angles = -2.0 * jnp.pi / length * turn_counts.astype(jnp.float32)
    return (jnp.cos(angles), jnp.sin(angles))


def pyramid(field_real, field_imag, gain_real, gain_imag):
    spectrum_real, spectrum_imag = transform(field_real, field_imag, -1.0)
    column_real = gain_real[None, :, None]
    column_imag = gain_imag[None, :, None]
    masked_real = spectrum_real * column_real - spectrum_imag * column_imag
    masked_imag = spectrum_real * column_imag + spectrum_imag * column_real
    back_real, back_imag = transform(masked_real, masked_imag, 1.0)
    inverse_length = 1.0 / field_real.shape[1]
    return (back_real * inverse_length, back_imag * inverse_length)


def row_ahead(field):
    return jnp.pad(field[:, :, 1:], ((0, 0), (0, 0), (0, 1)))


def row_behind(field):
    return jnp.pad(field[:, :, :-1], ((0, 0), (0, 0), (1, 0)))


def flow_terms(extended, frac_x, frac_r, first_frame, total_frames, first_pixel):
    frames_ext, width_ext, row_count = extended.shape
    frames_dev = frames_ext - 2
    near_x = jnp.pad(frac_x, ((1, 0), (0, 0)))
    near_r = jnp.pad(frac_r, ((1, 0), (0, 0)))
    stay_stay = (1.0 - near_x) * (1.0 - near_r)
    ahead_stay = near_x * (1.0 - near_r)
    stay_ahead = (1.0 - near_x) * near_r
    ahead_ahead = near_x * near_r
    base_cells = extended[:, :-1, :]
    ahead_cells = extended[:, 1:, :]
    moved = (
        stay_stay * base_cells
        + ahead_stay * ahead_cells
        + stay_ahead * row_ahead(base_cells)
        + ahead_ahead * row_ahead(ahead_cells)
    )
    flow = extended[1:, :-1, :] - moved[:-1]
    frame_ids = first_frame - 1 + lax.broadcasted_iota(jnp.int32, flow.shape, 0)
    pixel_ids = first_pixel - 1 + lax.broadcasted_iota(jnp.int32, flow.shape, 1)
    valid = (frame_ids >= 0) & (frame_ids <= total_frames - 2) & (pixel_ids >= 0)
    flow = jnp.where(valid, flow, 0.0)
    spread = (
        (stay_stay * flow)[:, 1:]
        + (ahead_stay * flow)[:, :-1]
        + row_behind((stay_ahead * flow)[:, 1:] + (ahead_ahead * flow)[:, :-1])
    )
    prior = flow[:frames_dev, 1:] - spread[1:]
    return (prior, flow[1:, 1:])


def forward_pass(full_phase, full_direction, tilts, amplitude, gain_real, gain_imag):
    frames_dev, pupil_width, row_count = full_phase.shape
    line_length = 2 * pupil_width
    quarter = pupil_width // 2
    local_points = tilts.shape[0]
    positions = quarter + jnp.arange(pupil_width, dtype=jnp.int32)
    tilt_turns = tilts[:, None] * positions[None, :] % line_length
    tilt_angles = 2.0 * jnp.pi / line_length * tilt_turns.astype(jnp.float32)
    angles = full_phase[None] + tilt_angles[:, None, :, None]
    field_real = amplitude * jnp.cos(angles)
    field_imag = amplitude * jnp.sin(angles)
    margins = ((0, 0), (quarter, quarter), (0, 0))
    line_batch = local_points * frames_dev

    def padded_lines(field):
        return jnp.pad(field.reshape(line_batch, pupil_width, row_count), margins)

    image_real, image_imag = pyramid(
        padded_lines(field_real), padded_lines(field_imag), gain_real, gain_imag
    )
    push_real, push_imag = pyramid(
        padded_lines(-field_imag * full_direction),
        padded_lines(field_real * full_direction),
        gain_real,
        gain_imag,
    )
    signal_terms = (2.0 * (image_real * push_real + image_imag * push_imag)).reshape(
        local_points, frames_dev, line_length, row_count
    )
    return (field_real, field_imag, image_real, image_imag, jnp.sum(signal_terms, axis=0))


def backward_pass(
    field_real, field_imag, image_real, image_imag, weighted_full, gain_real, gain_imag
):
    local_points, frames_dev, pupil_width, row_count = field_real.shape
    line_length = 2 * pupil_width
    quarter = pupil_width // 2
    line_batch = local_points * frames_dev
    image_shaped_real = image_real.reshape(local_points, frames_dev, line_length, row_count)
    image_shaped_imag = image_imag.reshape(local_points, frames_dev, line_length, row_count)
    source_real = (weighted_full[None] * image_shaped_real).reshape(
        line_batch, line_length, row_count
    )
    source_imag = (weighted_full[None] * image_shaped_imag).reshape(
        line_batch, line_length, row_count
    )
    back_real, back_imag = pyramid(source_real, source_imag, gain_real, -gain_imag)
    back_real = back_real[:, quarter : quarter + pupil_width].reshape(
        local_points, frames_dev, pupil_width, row_count
    )
    back_imag = back_imag[:, quarter : quarter + pupil_width].reshape(
        local_points, frames_dev, pupil_width, row_count
    )
    return -2.0 * jnp.sum(field_imag * back_real - field_real * back_imag, axis=0)


def per_device(phase, direction, pupil_mask, mod_tilts, wind_codes, noise_weight):
    frames_dev, shard_width, row_count = phase.shape
    mod_count = lax.axis_size("mod")
    pupil_width = shard_width * mod_count
    line_length = 2 * pupil_width
    quarter = pupil_width // 2
    mod_index = lax.axis_index("mod")
    first_frame = lax.axis_index("tm") * frames_dev
    total_frames = frames_dev * lax.axis_size("tm")
    first_pixel = mod_index * shard_width
    frac_x = ((wind_codes % 4).astype(jnp.float32) + 0.5) / 4.0
    frac_r = ((wind_codes // 4).astype(jnp.float32) + 0.5) / 4.0
    gain_real, gain_imag = roof_mask(line_length, quarter)
    rimmed = with_halo(direction, (("tm", 0),), 1)
    full_phase, full_rim = (
        lax.all_gather(phase, "mod", axis=1, tiled=True),
        lax.all_gather(rimmed, "mod", axis=1, tiled=True),
    )
    full_direction = full_rim[1:-1]
    extended = jnp.pad(full_rim, ((0, 0), (1, 1), (0, 0)))
    prior_lines, flow_lines = flow_terms(extended, frac_x, frac_r, first_frame, total_frames, 0)
    prior = lax.dynamic_slice_in_dim(prior_lines, first_pixel, shard_width, 1)
    amplitude = pupil_mask.astype(jnp.float32)
    field_real, field_imag, image_real, image_imag, signal_local = forward_pass(
        full_phase, full_direction, mod_tilts, amplitude, gain_real, gain_imag
    )
    signal_full = lax.psum(signal_local, "mod")
    weighted_used = noise_weight * signal_full
    grad_lines = backward_pass(
        field_real, field_imag, image_real, image_imag, weighted_used, gain_real, gain_imag
    )
    grad_own = lax.psum_scatter(grad_lines, "mod", scatter_dimension=1, tiled=True)
    hess_vec = grad_own + prior
    curvature_total = lax.psum(jnp.sum(direction * hess_vec), ("tm", "mod"))
    entry_count = float(total_frames * pupil_width * row_count)
    curvature = (curvature_total / entry_count).reshape(1)
    return (hess_vec, curvature)


TILE = 16
HALO = 8


def coupling_tables(pupil_width, pieces):
    per_piece = pupil_width // pieces
    order = [
        np.concatenate([pieces * np.arange(per_piece) + j for j in range(parity, pieces, 2)])
        for parity in (0, 1)
    ]
    tables = []
    for source in (0, 1):
        gap = order[1 - source][:, None] - order[source][None, :]
        exact = -1.0 / (pupil_width * np.sin(np.pi * gap / pupil_width))
        high = exact.astype(jnp.bfloat16)
        low = (exact - high.astype(np.float64)).astype(jnp.bfloat16)
        tables.append(np.concatenate([high, high, low], axis=1))
    return np.stack(tables)


def cos_sin(angle):
    turns = jnp.round(angle * np.float32(2.0 / np.pi))
    rest = angle - turns * np.float32(1.5703125)
    rest = rest - turns * np.float32(4.837512969970703125e-4)
    rest = rest - turns * np.float32(7.54978995489188216e-8)
    square = rest * rest
    sine = rest + rest * square * (
        np.float32(-1.6666654611e-1)
        + square * (np.float32(8.3321608736e-3) + square * np.float32(-1.9515295891e-4))
    )
    cosine = (
        1.0
        - 0.5 * square
        + square
        * square
        * (
            np.float32(4.166664568298827e-2)
            + square * (np.float32(-1.388731625493765e-3) + square * np.float32(2.443315711809948e-5))
        )
    )
    quarter = turns.astype(jnp.int32)
    swap = (quarter & 1) == 1
    out_cos = jnp.where(swap, sine, cosine)
    out_sin = jnp.where(swap, cosine, sine)
    out_cos = jnp.where(((quarter + 1) & 2) == 2, -out_cos, out_cos)
    out_sin = jnp.where((quarter & 2) == 2, -out_sin, out_sin)
    return out_cos, out_sin


def split(value):
    high = value.astype(jnp.bfloat16)
    return high, (value - high.astype(jnp.float32)).astype(jnp.bfloat16)


def fused_kernel(
    counts,
    phase_hbm,
    direction_hbm,
    tilts,
    mask_hbm,
    wind_hbm,
    noise_hbm,
    table_hbm,
    grads,
    prior,
    parts,
    send_lines,
    lines,
    send_tilt,
    tilt_tiles,
    extended,
    mask,
    wind,
    noise,
    table,
    packed_mask,
    packed_noise,
    turn,
    field,
    operand,
    image,
    push,
    dir_wide,
    bent,
    near,
    send_grad,
    phase,
    direction,
    local_sem,
    line_send,
    line_recv,
    halo_send,
    halo_recv,
    grad_send,
    grad_recv,
    part_send,
    part_recv,
    entered,
):
    tm_count, mod_count = counts
    frames, width, rows = phase.shape
    chunks = mod_count // frames
    chunk = rows // chunks
    pieces = chunks
    sub = width // pieces
    pupil = width * mod_count
    length = 2 * pupil
    packed_rows = pupil // pieces
    half = pupil // 2
    groups = mod_count // pieces
    lanes = groups * rows
    tm = lax.axis_index("tm")
    mod = lax.axis_index("mod")
    own_frame = mod // chunks
    own_chunk = mod % chunks

    copies = [
        pltpu.make_async_copy(noise_hbm.at[own_frame], noise, local_sem.at[0]),
        pltpu.make_async_copy(mask_hbm, mask, local_sem.at[1]),
        pltpu.make_async_copy(wind_hbm, wind, local_sem.at[2]),
        pltpu.make_async_copy(table_hbm, table, local_sem.at[3]),
        pltpu.make_async_copy(phase_hbm, phase, local_sem.at[4]),
        pltpu.make_async_copy(direction_hbm, direction, local_sem.at[5]),
    ]

    barrier = pltpu.get_barrier_semaphore()
    peers = [
        (a, b) for a in range(tm_count) for b in range(mod_count) if (a, b) != (0, 0)
    ]

    def peer(a, b):
        return {"tm": (tm + a) % tm_count, "mod": (mod + b) % mod_count}

    for b in range(1, mod_count):
        pl.semaphore_signal(
            barrier, inc=1, device_id=peer(0, b), device_id_type=pl.DeviceIdType.MESH
        )
    beside = [(-1, tm > 0), (1, tm < tm_count - 1)]

    def tell_beside(semaphores):
        for side, (step, exists) in enumerate(beside):

            @pl.when(exists)
            def _():
                pl.semaphore_signal(
                    semaphores[1 - side],
                    inc=1,
                    device_id=peer(step, 0),
                    device_id_type=pl.DeviceIdType.MESH,
                )

    def hear_beside(semaphores):
        for side, (step, exists) in enumerate(beside):

            @pl.when(exists)
            def _():
                pl.semaphore_wait(semaphores[side], 1)

    def entered_at(n):
        return [entered.at[n, 0], entered.at[n, 1]]

    tell_beside([barrier, barrier])
    for copy in copies[4:] + copies[:4]:
        copy.start()

    lane_group = lax.broadcasted_iota(jnp.int32, (TILE, rows), 1) // chunk

    def at_lanes(values):
        out_value = values[0]
        for j in range(1, len(values)):
            out_value = jnp.where(lane_group[: out_value.shape[0]] == j, values[j], out_value)
        return out_value

    def turned(value, amount):
        if isinstance(amount, int):
            amount = amount % rows
            if amount == 0:
                return value
        return pltpu.roll(value, amount, 1)

    def widened(value):
        shifts = [turned(value, s * chunk) for s in range(pieces)]
        return [
            at_lanes([shifts[(m - j) % pieces] for m in range(pieces)]) for j in range(pieces)
        ]

    def over_groups(value):
        step = chunk
        while step < rows:
            value = value + pltpu.roll(value, step, 1)
            step *= 2
        return value

    def tiles(n, body, unroll=2):
        def step(i, carry):
            body(pl.multiple_of(i * TILE, TILE))
            return carry

        lax.fori_loop(0, n // TILE, step, 0, unroll=unroll)

    for which, source in enumerate((phase, direction)):
        copies[4 + which].wait()
        for f in range(frames):
            for base in range(0, sub, TILE):
                loaded = [
                    source[f, pl.ds(base * pieces + j, TILE, stride=pieces), :]
                    for j in range(pieces)
                ]
                for k in range(chunks):
                    send_lines[which, f * chunks + k, base : base + TILE] = at_lanes(
                        [turned(loaded[j], (j - k) * chunk) for j in range(pieces)]
                    )

    send_tilt[...] = jnp.broadcast_to(tilts[...].astype(jnp.float32), send_tilt.shape)
    earlier, later = (tm + tm_count - 1) // tm_count, (2 * tm_count - 2 - tm) // tm_count
    pl.semaphore_wait(barrier, mod_count - 1 + earlier + later)

    my_lines = pl.ds(pl.multiple_of(mod * sub, sub), sub)
    tilt_copies, line_copies = [], [[], []]
    for o in range(1, mod_count):
        tilt_copies.append(
            pltpu.make_async_remote_copy(
                send_tilt,
                tilt_tiles.at[mod],
                line_send.at[2, o - 1],
                line_recv.at[2, o - 1],
                device_id=peer(0, o),
                device_id_type=pl.DeviceIdType.MESH,
            )
        )
        for which in range(2):
            line_copies[which].append(
                pltpu.make_async_remote_copy(
                    send_lines.at[which, (mod + o) % mod_count],
                    lines.at[which, my_lines],
                    line_send.at[which, o - 1],
                    line_recv.at[which, o - 1],
                    device_id=peer(0, o),
                    device_id_type=pl.DeviceIdType.MESH,
                )
            )
    for copy in tilt_copies + line_copies[0]:
        copy.start()
    tell_beside(entered_at(0))

    halos, corners = [], []
    for da in (-1, 0, 1):
        for db in (-1, 0, 1):
            if (da, db) == (0, 0):
                continue
            src_f, dst_f, n_f = {1: (frames - 1, 0, 1), 0: (0, 1, frames), -1: (0, frames + 1, 1)}[da]
            src_x, dst_x, n_x = {
                1: (width - HALO, 0, HALO),
                0: (0, HALO, width),
                -1: (0, HALO + width, HALO),
            }[db]
            slot = len(halos)
            copy = pltpu.make_async_remote_copy(
                direction.at[pl.ds(src_f, n_f), pl.ds(src_x, n_x)],
                extended.at[pl.ds(dst_f, n_f), pl.ds(dst_x, n_x)],
                halo_send.at[slot],
                halo_recv.at[slot],
                device_id=peer(da, db),
                device_id_type=pl.DeviceIdType.MESH,
            )
            sends = (tm + da >= 0) & (tm + da < tm_count) & (mod + db >= 0) & (mod + db < mod_count)
            takes = (tm - da >= 0) & (tm - da < tm_count) & (mod - db >= 0) & (mod - db < mod_count)
            halos.append((copy, sends, takes, (dst_f, n_f, dst_x, n_x)))
            if da == 0 or db == 0:
                pl.when(sends)(copy.start)
            else:
                corners.append((copy, sends))
    for copy in line_copies[1]:
        copy.start()

    for which in range(2):
        lines[which, my_lines] = send_lines[which, mod]
    tilt_tiles[mod] = send_tilt[...]
    extended[1 : 1 + frames, HALO : HALO + width] = direction[...]
    for _, _, takes, (dst_f, n_f, dst_x, n_x) in halos:

        @pl.when(jnp.logical_not(takes))
        def _():
            extended[dst_f : dst_f + n_f, dst_x : dst_x + n_x] = jnp.zeros(
                (n_f, n_x, rows), jnp.float32
            )

    copies[1].wait()
    copies[0].wait()

    def pack_own(source, base, row):
        return at_lanes(
            [
                pltpu.roll(
                    source[pl.ds(base + row * pieces + j, TILE, stride=pieces), :],
                    ((j + chunks - own_chunk) % chunks) * chunk,
                    1,
                )
                for j in range(pieces)
            ]
        )

    def pack_rows(row):
        packed_mask[pl.ds(row, TILE)] = pack_own(mask, 0, row).astype(jnp.float32)
        for side in range(2):
            packed_noise[side, pl.ds(row, TILE)] = pack_own(noise, side * pupil, row)

    tiles(packed_rows, pack_rows)

    hear_beside(entered_at(0))
    for copy, sends in corners:
        pl.when(sends)(copy.start)
    if tm_count > 2:
        tell_beside(entered_at(1))
    for copy in tilt_copies:
        copy.wait_recv()

    def turn_rows(row):
        for l in range(groups):
            tilt = at_lanes([tilt_tiles[l * pieces + m] for m in range(pieces)]).astype(jnp.int32)
            tilt = jnp.concatenate([tilt] * (TILE // tilt.shape[0]), axis=0)
            index = row + lax.broadcasted_iota(jnp.int32, (TILE, rows), 0)
            for j in range(pieces):
                position = half + pieces * index + j
                product = tilt * position
                if length & (length - 1) == 0:
                    product = product & (length - 1)
                else:
                    product = product % length
                cosine, sine = cos_sin(
                    np.float32(2.0 * np.pi / length) * product.astype(jnp.float32)
                )
                turn[0, j, pl.ds(row, TILE), l * rows : (l + 1) * rows] = cosine
                turn[1, j, pl.ds(row, TILE), l * rows : (l + 1) * rows] = sine

    tiles(packed_rows, turn_rows)

    def place(j, row):
        return j % 2, pl.ds(pl.multiple_of((j // 2) * packed_rows + row, TILE), TILE)

    def put_operand(j, row, l, real, imag):
        for part, value in enumerate((real, imag)):
            parity, _ = place(j, row)
            high, low = split(value)
            columns = slice(part * lanes + l * rows, part * lanes + (l + 1) * rows)
            start = (j // 2) * packed_rows + row
            for copy_index, item in enumerate((high, low, high)):
                operand[parity, pl.ds(pl.multiple_of(copy_index * half + start, TILE), TILE), columns] = item

    def couple(target):
        for parity in range(2):
            target[1 - parity] = jnp.dot(
                table[parity], operand[parity], preferred_element_type=jnp.float32
            )

    def columns_of(part, l):
        return slice(part * lanes + l * rows, part * lanes + (l + 1) * rows)

    for n in range(1, tm_count - 1):
        hear_beside(entered_at(n))
        if n < tm_count - 2:
            tell_beside(entered_at(n + 1))
    for copy in line_copies[0]:
        copy.wait_recv()

    def field_rows(row):
        cosine, sine = cos_sin(lines[0, pl.ds(row, TILE)])
        lit = packed_mask[pl.ds(row, TILE)]
        wide_cos, wide_sin = widened(cosine * lit), widened(sine * lit)
        for j in range(pieces):
            parity, where = place(j, row)
            for l in range(groups):
                turn_cos = turn[0, j, pl.ds(row, TILE), l * rows : (l + 1) * rows]
                turn_sin = turn[1, j, pl.ds(row, TILE), l * rows : (l + 1) * rows]
                real = wide_cos[j] * turn_cos - wide_sin[j] * turn_sin
                imag = wide_cos[j] * turn_sin + wide_sin[j] * turn_cos
                field[parity, where, columns_of(0, l)] = real
                field[parity, where, columns_of(1, l)] = imag
                put_operand(j, row, l, real, imag)

    tiles(packed_rows, field_rows)
    copies[3].wait()
    couple(image)

    copies[2].wait()
    for copy, _, takes, _ in halos:
        pl.when(takes)(copy.wait_recv)
    before = pl.ds(
        pl.multiple_of(((mod + mod_count - 1) % mod_count) * width + (width - HALO), HALO), HALO
    )
    codes = jnp.concatenate(
        [wind[before], wind[pl.ds(pl.multiple_of(mod * width, HALO), width)]], axis=0
    )
    tall = HALO + width
    frac_x = ((codes & 3).astype(jnp.float32) + 0.5) * 0.25
    frac_r = ((codes >> 2).astype(jnp.float32) + 0.5) * 0.25
    stay_stay = (1.0 - frac_x) * (1.0 - frac_r)
    ahead_stay = frac_x * (1.0 - frac_r)
    stay_ahead = (1.0 - frac_x) * frac_r
    ahead_ahead = frac_x * frac_r
    lane = lax.broadcasted_iota(jnp.int32, (tall, rows), 1)
    pixel = mod * width - HALO + lax.broadcasted_iota(jnp.int32, (tall, rows), 0)
    total_frames = frames * tm_count
    flow_power = jnp.zeros((HALO, rows), jnp.float32)
    for i in range(frames + 1):
        base = extended[i, 0:tall]
        ahead = extended[i, 1 : tall + 1]
        crossing = stay_ahead * jnp.where(lane == rows - 1, 0.0, pltpu.roll(base, rows - 1, 1))
        crossing += ahead_ahead * jnp.where(lane == rows - 1, 0.0, pltpu.roll(ahead, rows - 1, 1))
        moved = stay_stay * base + ahead_stay * ahead + crossing
        flow_id = tm * frames - 1 + i
        valid = (pixel >= 0) & (flow_id >= 0) & (flow_id <= total_frames - 2)
        flow = jnp.where(valid, extended[i + 1, 0:tall] - moved, 0.0)
        if i >= 1:
            for start in range(HALO, tall, HALO):
                flow_power += flow[start : start + HALO] * flow[start : start + HALO]
            near[0] = ahead_stay * flow
            near[1] = ahead_ahead * flow
            behind = (stay_ahead * flow)[HALO:] + near[1, HALO - 1 : HALO - 1 + width]
            spread = (
                (stay_stay * flow)[HALO:]
                + near[0, HALO - 1 : HALO - 1 + width]
                + jnp.where(lane[HALO:] == 0, 0.0, pltpu.roll(behind, 1, 1))
            )
            prior[i - 1] = prior[i - 1] - spread
        if i < frames:
            prior[i] = flow[HALO:]

    for copy in line_copies[1]:
        copy.wait_recv()

    def dir_rows(row):
        wide = widened(lines[1, pl.ds(row, TILE)])
        for j in range(pieces):
            parity, where = place(j, row)
            dir_wide[parity, where] = wide[j]
            for l in range(groups):
                real = field[parity, where, columns_of(0, l)] * wide[j]
                imag = field[parity, where, columns_of(1, l)] * wide[j]
                put_operand(j, row, l, real, imag)

    tiles(packed_rows, dir_rows)
    couple(push)

    def signal_rows(i, power):
        row = pl.multiple_of(i * TILE, TILE)
        wide_noise = [widened(packed_noise[side, pl.ds(row, TILE)]) for side in range(2)]
        for j in range(pieces):
            parity, where = place(j, row)
            step = dir_wide[parity, where]
            even = odd = None
            for l in range(groups):
                er = field[parity, where, columns_of(0, l)]
                ei = field[parity, where, columns_of(1, l)]
                ur = image[parity, where, columns_of(0, l)]
                ui = image[parity, where, columns_of(1, l)]
                vr = push[parity, where, columns_of(0, l)]
                vi = push[parity, where, columns_of(1, l)]
                even_l = ui * vr - ur * vi
                odd_l = (ur * er + ui * ei) * step - (er * vr + ei * vi)
                even = even_l if even is None else even + even_l
                odd = odd_l if odd is None else odd + odd_l
            even = 2.0 * over_groups(even)
            odd = over_groups(odd)
            front = wide_noise[0][j] * (even + odd)
            back = wide_noise[1][j] * (even - odd)
            power = power + front * (even + odd) + back * (even - odd)
            both = front + back
            differ = 0.5 * (front - back)
            bent[parity, where] = differ
            for l in range(groups):
                er = field[parity, where, columns_of(0, l)]
                ei = field[parity, where, columns_of(1, l)]
                ur = image[parity, where, columns_of(0, l)]
                ui = image[parity, where, columns_of(1, l)]
                put_operand(j, row, l, differ * er - both * ui, differ * ei + both * ur)

        return power

    power = lax.fori_loop(
        0, packed_rows // TILE, signal_rows, jnp.zeros((TILE, rows), jnp.float32), unroll=2
    )
    parts_own = tm * mod_count + mod
    parts[parts_own] = (power[:HALO] + power[HALO:]) * (1.0 / pieces) + flow_power
    part_copies = []
    for slot, (a, b) in enumerate(peers):
        part_copies.append(
            pltpu.make_async_remote_copy(
                parts.at[parts_own],
                parts.at[parts_own],
                part_send.at[slot],
                part_recv.at[slot],
                device_id=peer(a, b),
                device_id_type=pl.DeviceIdType.MESH,
            )
        )
        part_copies[-1].start()
    couple(push)

    def grad_rows(row):
        grad = []
        for j in range(pieces):
            parity, where = place(j, row)
            differ = bent[parity, where]
            acc = None
            for l in range(groups):
                er = field[parity, where, columns_of(0, l)]
                ei = field[parity, where, columns_of(1, l)]
                kr = differ * image[parity, where, columns_of(0, l)] + push[parity, where, columns_of(0, l)]
                ki = differ * image[parity, where, columns_of(1, l)] + push[parity, where, columns_of(1, l)]
                term = er * kr + ei * ki
                acc = term if acc is None else acc + term
            grad.append(2.0 * over_groups(acc))
        send_grad[pl.ds(row, TILE)] = at_lanes(grad)

    tiles(packed_rows, grad_rows)

    grad_copies = []
    for o in range(1, mod_count):
        owner = (mod + o) % mod_count
        grad_copies.append(
            pltpu.make_async_remote_copy(
                send_grad.at[pl.ds(pl.multiple_of(owner * sub, sub), sub)],
                grads.at[mod],
                grad_send.at[o - 1],
                grad_recv.at[o - 1],
                device_id=peer(0, o),
                device_id_type=pl.DeviceIdType.MESH,
            )
        )
        grad_copies[-1].start()
    grads[mod] = send_grad[my_lines]

    for copy in tilt_copies + line_copies[0] + line_copies[1]:
        copy.wait_send()
    for copy, sends, _, _ in halos:
        pl.when(sends)(copy.wait_send)
    for copy in grad_copies + part_copies:
        copy.wait()


def gather_kernel(entries, grads, prior, parts, out, curvature):
    frames, width, rows = prior.shape
    mod_count, sub, _ = grads.shape
    pieces = mod_count // frames
    chunk = rows // pieces
    lane_group = lax.broadcasted_iota(jnp.int32, (TILE, rows), 1) // chunk
    for f in range(frames):
        for base in range(0, sub, TILE):
            arrived = [grads[f * pieces + k, base : base + TILE] for k in range(pieces)]
            for j in range(pieces):
                where = pl.ds(base * pieces + j, TILE, stride=pieces)
                grad = None
                for k in range(pieces):
                    shift = (k - j) * chunk % rows
                    piece = pltpu.roll(arrived[k], shift, 1) if shift else arrived[k]
                    grad = piece if grad is None else jnp.where(lane_group == k, piece, grad)
                out[f, where, :] = grad + prior[f, where, :]
    whole = parts[0]
    for n in range(1, parts.shape[0]):
        whole = whole + parts[n]
    curvature[0] = jnp.sum(whole) / entries


def fused_device(phase, direction, pupil_mask, mod_tilts, wind_codes, noise_weight):
    frames, width, rows = phase.shape
    tm_count, mod_count = lax.axis_size("tm"), lax.axis_size("mod")
    pieces = mod_count // frames
    sub = width // pieces
    pupil = width * mod_count
    half = pupil // 2
    lanes = mod_count // pieces * rows
    packed_rows = pupil // pieces
    everyone = tm_count * mod_count
    vmem, smem, hbm = (
        pl.BlockSpec(memory_space=pltpu.VMEM),
        pl.BlockSpec(memory_space=pltpu.SMEM),
        pl.BlockSpec(memory_space=pl.ANY),
    )
    f32, bf16 = jnp.float32, jnp.bfloat16
    dma = pltpu.SemaphoreType.DMA
    sums = pl.pallas_call(
        functools.partial(fused_kernel, (tm_count, mod_count)),
        out_shape=(
            pltpu.VMEM((mod_count, sub, rows), f32),
            pltpu.VMEM(phase.shape, f32),
            pltpu.VMEM((everyone, HALO, rows), f32),
        ),
        in_specs=[hbm, hbm, vmem, hbm, hbm, hbm, hbm],
        out_specs=(vmem, vmem, vmem),
        scratch_shapes=[
            pltpu.VMEM((2, mod_count, sub, rows), f32),
            pltpu.VMEM((2, packed_rows, rows), f32),
            pltpu.VMEM((8, rows), f32),
            pltpu.VMEM((mod_count, 8, rows), f32),
            pltpu.VMEM((frames + 2, width + 2 * HALO, rows), f32),
            pltpu.VMEM(pupil_mask.shape, jnp.int32),
            pltpu.VMEM(wind_codes.shape, jnp.int32),
            pltpu.VMEM(noise_weight.shape[1:], f32),
            pltpu.VMEM((2, half, 3 * half), bf16),
            pltpu.VMEM((packed_rows, rows), f32),
            pltpu.VMEM((2, packed_rows, rows), f32),
            pltpu.VMEM((2, pieces, packed_rows, lanes), f32),
            pltpu.VMEM((2, half, 2 * lanes), f32),
            pltpu.VMEM((2, 3 * half, 2 * lanes), bf16),
            pltpu.VMEM((2, half, 2 * lanes), f32),
            pltpu.VMEM((2, half, 2 * lanes), f32),
            pltpu.VMEM((2, half, rows), f32),
            pltpu.VMEM((2, half, rows), f32),
            pltpu.VMEM((2, width + HALO, rows), f32),
            pltpu.VMEM((packed_rows, rows), f32),
            pltpu.VMEM(phase.shape, f32),
            pltpu.VMEM(direction.shape, f32),
            dma((6,)),
            dma((3, mod_count - 1)),
            dma((3, mod_count - 1)),
            dma((8,)),
            dma((8,)),
            dma((mod_count - 1,)),
            dma((mod_count - 1,)),
            dma((everyone - 1,)),
            dma((everyone - 1,)),
            pltpu.SemaphoreType.REGULAR((max(tm_count - 1, 1), 2)),
        ],
        compiler_params=pltpu.CompilerParams(collective_id=0, has_side_effects=True),
    )(
        phase,
        direction,
        mod_tilts.reshape(1, 1),
        pupil_mask,
        wind_codes,
        noise_weight,
        jnp.asarray(coupling_tables(pupil, pieces)),
    )
    return pl.pallas_call(
        functools.partial(gather_kernel, float(frames * tm_count * pupil * rows)),
        out_shape=(jax.ShapeDtypeStruct(phase.shape, f32), jax.ShapeDtypeStruct((1,), f32)),
        in_specs=[vmem, vmem, vmem],
        out_specs=(vmem, smem),
    )(*[pltpu.with_memory_space_constraint(item, pltpu.VMEM) for item in sums])


def device_program(phase, direction, pupil_mask, mod_tilts, wind_codes, noise_weight):
    frames, width, rows = phase.shape
    mod_count = lax.axis_size("mod")
    fits = mod_count % frames == 0 and mod_tilts.shape[0] == 1 and frames > 1
    if fits:
        pieces = mod_count // frames
        fits = (
            lax.axis_size("tm") > 1
            and pieces % 2 == 0
            and rows == 128
            and rows % pieces == 0
            and width % (pieces * TILE) == 0
            and pieces & (pieces - 1) == 0
        )
    run = fused_device if fits else per_device
    return run(phase, direction, pupil_mask, mod_tilts, wind_codes, noise_weight)


def solution(mesh):
    return jax.shard_map(
        device_program,
        mesh=mesh,
        in_specs=(
            P(("grp", "tm"), "mod", None),
            P(("grp", "tm"), "mod", None),
            P(),
            P("mod"),
            P("grp", None),
            P(("grp", "tm"), None, None),
        ),
        out_specs=(P(("grp", "tm"), "mod", None), P("grp")),
        check_vma=False,
    )
```

```python
import functools

import jax
import jax.numpy as jnp
import numpy as np
from jax import lax
from jax.experimental import pallas as pl
from jax.experimental.pallas import tpu as pltpu
from jax.sharding import PartitionSpec as P

HIGHEST = lax.Precision.HIGHEST


def with_halo(cells, sides, width):
    for axis, dim in sides:
        count = lax.axis_size(axis)
        ends = count - 1
        head = lax.slice_in_dim(cells, 0, width, axis=dim)
        tail = lax.slice_in_dim(cells, cells.shape[dim] - width, cells.shape[dim], axis=dim)
        cells = jnp.concatenate(
            [
                lax.ppermute(tail, axis, [(i, (i + 1) % count) for i in range(ends)]),
                cells,
                lax.ppermute(head, axis, [((i + 1) % count, i) for i in range(ends)]),
            ],
            axis=dim,
        )
    return cells


def square_table(count, orient):
    index_range = jnp.arange(count, dtype=jnp.int32)
    turn_counts = index_range[:, None] * index_range[None, :] % count
    angles = orient * 2.0 * jnp.pi / count * turn_counts.astype(jnp.float32)
    return (jnp.cos(angles), jnp.sin(angles))


def complex_mix(form, table_real, table_imag, field_real, field_imag):
    real_real = jnp.einsum(form, table_real, field_real, precision=HIGHEST)
    imag_imag = jnp.einsum(form, table_imag, field_imag, precision=HIGHEST)
    real_imag = jnp.einsum(form, table_real, field_imag, precision=HIGHEST)
    imag_real = jnp.einsum(form, table_imag, field_real, precision=HIGHEST)
    return (real_real - imag_imag, real_imag + imag_real)


def transform(field_real, field_imag, orient):
    batch_size, length, row_count = field_real.shape
    outer_size = 32
    inner_size = length // outer_size
    first_real, first_imag = square_table(outer_size, orient)
    second_real, second_imag = square_table(inner_size, orient)
    turn_counts = (
        jnp.arange(outer_size, dtype=jnp.int32)[:, None]
        * jnp.arange(inner_size, dtype=jnp.int32)[None, :]
        % length
    )
    angles = orient * 2.0 * jnp.pi / length * turn_counts.astype(jnp.float32)
    twist_real = jnp.cos(angles)[None, :, :, None]
    twist_imag = jnp.sin(angles)[None, :, :, None]
    shaped_real = field_real.reshape(batch_size, outer_size, inner_size, row_count)
    shaped_imag = field_imag.reshape(batch_size, outer_size, inner_size, row_count)
    section_real, section_imag = complex_mix(
        "kn,bnmr->bkmr", first_real, first_imag, shaped_real, shaped_imag
    )
    turned_real = section_real * twist_real - section_imag * twist_imag
    turned_imag = section_real * twist_imag + section_imag * twist_real
    final_real, final_imag = complex_mix(
        "dm,bkmr->bdkr", second_real, second_imag, turned_real, turned_imag
    )
    return (
        final_real.reshape(batch_size, length, row_count),
        final_imag.reshape(batch_size, length, row_count),
    )


def roof_mask(length, shift_bins):
    freq_index = jnp.arange(length, dtype=jnp.int32)
    signed_freq = jnp.where(freq_index < length // 2, freq_index, freq_index - length)
    turn_counts = shift_bins * jnp.abs(signed_freq) % length
    angles = -2.0 * jnp.pi / length * turn_counts.astype(jnp.float32)
    return (jnp.cos(angles), jnp.sin(angles))


def pyramid(field_real, field_imag, gain_real, gain_imag):
    spectrum_real, spectrum_imag = transform(field_real, field_imag, -1.0)
    column_real = gain_real[None, :, None]
    column_imag = gain_imag[None, :, None]
    masked_real = spectrum_real * column_real - spectrum_imag * column_imag
    masked_imag = spectrum_real * column_imag + spectrum_imag * column_real
    back_real, back_imag = transform(masked_real, masked_imag, 1.0)
    inverse_length = 1.0 / field_real.shape[1]
    return (back_real * inverse_length, back_imag * inverse_length)


def row_ahead(field):
    return jnp.pad(field[:, :, 1:], ((0, 0), (0, 0), (0, 1)))


def row_behind(field):
    return jnp.pad(field[:, :, :-1], ((0, 0), (0, 0), (1, 0)))


def flow_terms(extended, frac_x, frac_r, first_frame, total_frames, first_pixel):
    frames_ext, width_ext, row_count = extended.shape
    frames_dev = frames_ext - 2
    near_x = jnp.pad(frac_x, ((1, 0), (0, 0)))
    near_r = jnp.pad(frac_r, ((1, 0), (0, 0)))
    stay_stay = (1.0 - near_x) * (1.0 - near_r)
    ahead_stay = near_x * (1.0 - near_r)
    stay_ahead = (1.0 - near_x) * near_r
    ahead_ahead = near_x * near_r
    base_cells = extended[:, :-1, :]
    ahead_cells = extended[:, 1:, :]
    moved = (
        stay_stay * base_cells
        + ahead_stay * ahead_cells
        + stay_ahead * row_ahead(base_cells)
        + ahead_ahead * row_ahead(ahead_cells)
    )
    flow = extended[1:, :-1, :] - moved[:-1]
    frame_ids = first_frame - 1 + lax.broadcasted_iota(jnp.int32, flow.shape, 0)
    pixel_ids = first_pixel - 1 + lax.broadcasted_iota(jnp.int32, flow.shape, 1)
    valid = (frame_ids >= 0) & (frame_ids <= total_frames - 2) & (pixel_ids >= 0)
    flow = jnp.where(valid, flow, 0.0)
    spread = (
        (stay_stay * flow)[:, 1:]
        + (ahead_stay * flow)[:, :-1]
        + row_behind((stay_ahead * flow)[:, 1:] + (ahead_ahead * flow)[:, :-1])
    )
    prior = flow[:frames_dev, 1:] - spread[1:]
    return (prior, flow[1:, 1:])


def forward_pass(full_phase, full_direction, tilts, amplitude, gain_real, gain_imag):
    frames_dev, pupil_width, row_count = full_phase.shape
    line_length = 2 * pupil_width
    quarter = pupil_width // 2
    local_points = tilts.shape[0]
    positions = quarter + jnp.arange(pupil_width, dtype=jnp.int32)
    tilt_turns = tilts[:, None] * positions[None, :] % line_length
    tilt_angles = 2.0 * jnp.pi / line_length * tilt_turns.astype(jnp.float32)
    angles = full_phase[None] + tilt_angles[:, None, :, None]
    field_real = amplitude * jnp.cos(angles)
    field_imag = amplitude * jnp.sin(angles)
    margins = ((0, 0), (quarter, quarter), (0, 0))
    line_batch = local_points * frames_dev

    def padded_lines(field):
        return jnp.pad(field.reshape(line_batch, pupil_width, row_count), margins)

    image_real, image_imag = pyramid(
        padded_lines(field_real), padded_lines(field_imag), gain_real, gain_imag
    )
    push_real, push_imag = pyramid(
        padded_lines(-field_imag * full_direction),
        padded_lines(field_real * full_direction),
        gain_real,
        gain_imag,
    )
    signal_terms = (2.0 * (image_real * push_real + image_imag * push_imag)).reshape(
        local_points, frames_dev, line_length, row_count
    )
    return (field_real, field_imag, image_real, image_imag, jnp.sum(signal_terms, axis=0))


def backward_pass(
    field_real, field_imag, image_real, image_imag, weighted_full, gain_real, gain_imag
):
    local_points, frames_dev, pupil_width, row_count = field_real.shape
    line_length = 2 * pupil_width
    quarter = pupil_width // 2
    line_batch = local_points * frames_dev
    image_shaped_real = image_real.reshape(local_points, frames_dev, line_length, row_count)
    image_shaped_imag = image_imag.reshape(local_points, frames_dev, line_length, row_count)
    source_real = (weighted_full[None] * image_shaped_real).reshape(
        line_batch, line_length, row_count
    )
    source_imag = (weighted_full[None] * image_shaped_imag).reshape(
        line_batch, line_length, row_count
    )
    back_real, back_imag = pyramid(source_real, source_imag, gain_real, -gain_imag)
    back_real = back_real[:, quarter : quarter + pupil_width].reshape(
        local_points, frames_dev, pupil_width, row_count
    )
    back_imag = back_imag[:, quarter : quarter + pupil_width].reshape(
        local_points, frames_dev, pupil_width, row_count
    )
    return -2.0 * jnp.sum(field_imag * back_real - field_real * back_imag, axis=0)


def per_device(phase, direction, pupil_mask, mod_tilts, wind_codes, noise_weight):
    frames_dev, shard_width, row_count = phase.shape
    mod_count = lax.axis_size("mod")
    pupil_width = shard_width * mod_count
    line_length = 2 * pupil_width
    quarter = pupil_width // 2
    mod_index = lax.axis_index("mod")
    first_frame = lax.axis_index("tm") * frames_dev
    total_frames = frames_dev * lax.axis_size("tm")
    first_pixel = mod_index * shard_width
    frac_x = ((wind_codes % 4).astype(jnp.float32) + 0.5) / 4.0
    frac_r = ((wind_codes // 4).astype(jnp.float32) + 0.5) / 4.0
    gain_real, gain_imag = roof_mask(line_length, quarter)
    rimmed = with_halo(direction, (("tm", 0),), 1)
    full_phase, full_rim = (
        lax.all_gather(phase, "mod", axis=1, tiled=True),
        lax.all_gather(rimmed, "mod", axis=1, tiled=True),
    )
    full_direction = full_rim[1:-1]
    extended = jnp.pad(full_rim, ((0, 0), (1, 1), (0, 0)))
    prior_lines, flow_lines = flow_terms(extended, frac_x, frac_r, first_frame, total_frames, 0)
    prior = lax.dynamic_slice_in_dim(prior_lines, first_pixel, shard_width, 1)
    amplitude = pupil_mask.astype(jnp.float32)
    field_real, field_imag, image_real, image_imag, signal_local = forward_pass(
        full_phase, full_direction, mod_tilts, amplitude, gain_real, gain_imag
    )
    signal_full = lax.psum(signal_local, "mod")
    weighted_used = noise_weight * signal_full
    grad_lines = backward_pass(
        field_real, field_imag, image_real, image_imag, weighted_used, gain_real, gain_imag
    )
    grad_own = lax.psum_scatter(grad_lines, "mod", scatter_dimension=1, tiled=True)
    hess_vec = grad_own + prior
    curvature_total = lax.psum(jnp.sum(direction * hess_vec), ("tm", "mod"))
    entry_count = float(total_frames * pupil_width * row_count)
    curvature = (curvature_total / entry_count).reshape(1)
    return (hess_vec, curvature)


TILE = 16
HALO = 8


def coupling_tables(pupil_width, pieces):
    per_piece = pupil_width // pieces
    order = [
        np.concatenate([pieces * np.arange(per_piece) + j for j in range(parity, pieces, 2)])
        for parity in (0, 1)
    ]
    tables = []
    for source in (0, 1):
        gap = order[1 - source][:, None] - order[source][None, :]
        exact = -1.0 / (pupil_width * np.sin(np.pi * gap / pupil_width))
        high = exact.astype(jnp.bfloat16)
        low = (exact - high.astype(np.float64)).astype(jnp.bfloat16)
        tables.append(np.concatenate([high, high, low], axis=1))
    return np.stack(tables)


def cos_sin(angle):
    turns = jnp.round(angle * np.float32(2.0 / np.pi))
    rest = angle - turns * np.float32(1.5703125)
    rest = rest - turns * np.float32(4.837512969970703125e-4)
    rest = rest - turns * np.float32(7.54978995489188216e-8)
    square = rest * rest
    sine = rest + rest * square * (
        np.float32(-1.6666654611e-1)
        + square * (np.float32(8.3321608736e-3) + square * np.float32(-1.9515295891e-4))
    )
    cosine = (
        1.0
        - 0.5 * square
        + square
        * square
        * (
            np.float32(4.166664568298827e-2)
            + square * (np.float32(-1.388731625493765e-3) + square * np.float32(2.443315711809948e-5))
        )
    )
    quarter = turns.astype(jnp.int32)
    swap = (quarter & 1) == 1
    out_cos = jnp.where(swap, sine, cosine)
    out_sin = jnp.where(swap, cosine, sine)
    out_cos = jnp.where(((quarter + 1) & 2) == 2, -out_cos, out_cos)
    out_sin = jnp.where((quarter & 2) == 2, -out_sin, out_sin)
    return out_cos, out_sin


def split(value):
    high = value.astype(jnp.bfloat16)
    return high, (value - high.astype(jnp.float32)).astype(jnp.bfloat16)


def fused_kernel(
    counts,
    phase_hbm,
    direction_hbm,
    tilts,
    mask_hbm,
    wind_hbm,
    noise_hbm,
    table_hbm,
    grads,
    prior,
    parts,
    send_lines,
    lines,
    send_tilt,
    tilt_tiles,
    extended,
    mask,
    wind,
    noise,
    table,
    packed_mask,
    noise_wide,
    turn,
    field,
    operand,
    image,
    push,
    dir_wide,
    bent,
    near,
    send_grad,
    phase,
    direction,
    local_sem,
    line_send,
    line_recv,
    halo_send,
    halo_recv,
    grad_send,
    grad_recv,
    part_send,
    part_recv,
    entered,
):
    tm_count, mod_count = counts
    frames, width, rows = phase.shape
    chunks = mod_count // frames
    chunk = rows // chunks
    pieces = chunks
    sub = width // pieces
    pupil = width * mod_count
    length = 2 * pupil
    packed_rows = pupil // pieces
    half = pupil // 2
    groups = mod_count // pieces
    lanes = groups * rows
    tm = lax.axis_index("tm")
    mod = lax.axis_index("mod")
    own_frame = mod // chunks
    own_chunk = mod % chunks

    copies = [
        pltpu.make_async_copy(noise_hbm.at[own_frame], noise, local_sem.at[0]),
        pltpu.make_async_copy(mask_hbm, mask, local_sem.at[1]),
        pltpu.make_async_copy(wind_hbm, wind, local_sem.at[2]),
        pltpu.make_async_copy(table_hbm, table, local_sem.at[3]),
        pltpu.make_async_copy(phase_hbm, phase, local_sem.at[4]),
        pltpu.make_async_copy(direction_hbm, direction, local_sem.at[5]),
    ]

    barrier = pltpu.get_barrier_semaphore()
    peers = [
        (a, b) for a in range(tm_count) for b in range(mod_count) if (a, b) != (0, 0)
    ]

    def peer(a, b):
        return {"tm": (tm + a) % tm_count, "mod": (mod + b) % mod_count}

    for b in range(1, mod_count):
        pl.semaphore_signal(
            barrier, inc=1, device_id=peer(0, b), device_id_type=pl.DeviceIdType.MESH
        )
    beside = [(-1, tm > 0), (1, tm < tm_count - 1)]

    def tell_beside(semaphores):
        for side, (step, exists) in enumerate(beside):

            @pl.when(exists)
            def _():
                pl.semaphore_signal(
                    semaphores[1 - side],
                    inc=1,
                    device_id=peer(step, 0),
                    device_id_type=pl.DeviceIdType.MESH,
                )

    def hear_beside(semaphores):
        for side, (step, exists) in enumerate(beside):

            @pl.when(exists)
            def _():
                pl.semaphore_wait(semaphores[side], 1)

    def entered_at(n):
        return [entered.at[n, 0], entered.at[n, 1]]

    tell_beside([barrier, barrier])
    for copy in copies[4:] + copies[:4]:
        copy.start()

    lane_group = lax.broadcasted_iota(jnp.int32, (TILE, rows), 1) // chunk

    def at_lanes(values):
        out_value = values[0]
        for j in range(1, len(values)):
            out_value = jnp.where(lane_group[: out_value.shape[0]] == j, values[j], out_value)
        return out_value

    def turned(value, amount):
        if isinstance(amount, int):
            amount = amount % rows
            if amount == 0:
                return value
        return pltpu.roll(value, amount, 1)

    def widened(value):
        shifts = [turned(value, s * chunk) for s in range(pieces)]
        return [
            at_lanes([shifts[(m - j) % pieces] for m in range(pieces)]) for j in range(pieces)
        ]

    def over_groups(value):
        step = chunk
        while step < rows:
            value = value + pltpu.roll(value, step, 1)
            step *= 2
        return value

    def tiles(n, body, unroll=2):
        def step(i, carry):
            body(pl.multiple_of(i * TILE, TILE))
            return carry

        lax.fori_loop(0, n // TILE, step, 0, unroll=unroll)

    for which, source in enumerate((phase, direction)):
        copies[4 + which].wait()
        for f in range(frames):
            for base in range(0, sub, TILE):
                loaded = [
                    source[f, pl.ds(base * pieces + j, TILE, stride=pieces), :]
                    for j in range(pieces)
                ]
                for k in range(chunks):
                    send_lines[which, f * chunks + k, base : base + TILE] = at_lanes(
                        [turned(loaded[j], (j - k) * chunk) for j in range(pieces)]
                    )

    send_tilt[...] = jnp.broadcast_to(tilts[...].astype(jnp.float32), send_tilt.shape)
    earlier, later = (tm + tm_count - 1) // tm_count, (2 * tm_count - 2 - tm) // tm_count
    pl.semaphore_wait(barrier, mod_count - 1 + earlier + later)

    my_lines = pl.ds(pl.multiple_of(mod * sub, sub), sub)
    tilt_copies, line_copies = [], [[], []]
    for o in range(1, mod_count):
        tilt_copies.append(
            pltpu.make_async_remote_copy(
                send_tilt,
                tilt_tiles.at[mod],
                line_send.at[2, o - 1],
                line_recv.at[2, o - 1],
                device_id=peer(0, o),
                device_id_type=pl.DeviceIdType.MESH,
            )
        )
        for which in range(2):
            line_copies[which].append(
                pltpu.make_async_remote_copy(
                    send_lines.at[which, (mod + o) % mod_count],
                    lines.at[which, my_lines],
                    line_send.at[which, o - 1],
                    line_recv.at[which, o - 1],
                    device_id=peer(0, o),
                    device_id_type=pl.DeviceIdType.MESH,
                )
            )
    for copy in tilt_copies + line_copies[0]:
        copy.start()
    tell_beside(entered_at(0))

    halos, corners = [], []
    for da in (-1, 0, 1):
        for db in (-1, 0, 1):
            if (da, db) == (0, 0):
                continue
            src_f, dst_f, n_f = {1: (frames - 1, 0, 1), 0: (0, 1, frames), -1: (0, frames + 1, 1)}[da]
            src_x, dst_x, n_x = {
                1: (width - HALO, 0, HALO),
                0: (0, HALO, width),
                -1: (0, HALO + width, HALO),
            }[db]
            slot = len(halos)
            copy = pltpu.make_async_remote_copy(
                direction.at[pl.ds(src_f, n_f), pl.ds(src_x, n_x)],
                extended.at[pl.ds(dst_f, n_f), pl.ds(dst_x, n_x)],
                halo_send.at[slot],
                halo_recv.at[slot],
                device_id=peer(da, db),
                device_id_type=pl.DeviceIdType.MESH,
            )
            sends = (tm + da >= 0) & (tm + da < tm_count) & (mod + db >= 0) & (mod + db < mod_count)
            takes = (tm - da >= 0) & (tm - da < tm_count) & (mod - db >= 0) & (mod - db < mod_count)
            halos.append((copy, sends, takes, (dst_f, n_f, dst_x, n_x)))
            if da == 0 or db == 0:
                pl.when(sends)(copy.start)
            else:
                corners.append((copy, sends))
    for copy in line_copies[1]:
        copy.start()

    for which in range(2):
        lines[which, my_lines] = send_lines[which, mod]
    tilt_tiles[mod] = send_tilt[...]
    extended[1 : 1 + frames, HALO : HALO + width] = direction[...]
    for _, _, takes, (dst_f, n_f, dst_x, n_x) in halos:

        @pl.when(jnp.logical_not(takes))
        def _():
            extended[dst_f : dst_f + n_f, dst_x : dst_x + n_x] = jnp.zeros(
                (n_f, n_x, rows), jnp.float32
            )

    copies[1].wait()
    copies[0].wait()

    def pack_own(source, base, row):
        return at_lanes(
            [
                pltpu.roll(
                    source[pl.ds(base + row * pieces + j, TILE, stride=pieces), :],
                    ((j + chunks - own_chunk) % chunks) * chunk,
                    1,
                )
                for j in range(pieces)
            ]
        )

    def place(j, row):
        return j % 2, pl.ds(pl.multiple_of((j // 2) * packed_rows + row, TILE), TILE)

    def pack_rows(row):
        packed_mask[pl.ds(row, TILE)] = pack_own(mask, 0, row).astype(jnp.float32)
        for side in range(2):
            wide = widened(pack_own(noise, side * pupil, row))
            for j in range(pieces):
                parity, where = place(j, row)
                noise_wide[side, parity, where] = wide[j]

    tiles(packed_rows, pack_rows)

    hear_beside(entered_at(0))
    for copy, sends in corners:
        pl.when(sends)(copy.start)
    if tm_count > 2:
        tell_beside(entered_at(1))
    for copy in tilt_copies:
        copy.wait_recv()

    def turn_rows(row):
        for l in range(groups):
            tilt = at_lanes([tilt_tiles[l * pieces + m] for m in range(pieces)]).astype(jnp.int32)
            tilt = jnp.concatenate([tilt] * (TILE // tilt.shape[0]), axis=0)
            index = row + lax.broadcasted_iota(jnp.int32, (TILE, rows), 0)
            for j in range(pieces):
                position = half + pieces * index + j
                product = tilt * position
                if length & (length - 1) == 0:
                    product = product & (length - 1)
                else:
                    product = product % length
                cosine, sine = cos_sin(
                    np.float32(2.0 * np.pi / length) * product.astype(jnp.float32)
                )
                turn[0, j, pl.ds(row, TILE), l * rows : (l + 1) * rows] = cosine
                turn[1, j, pl.ds(row, TILE), l * rows : (l + 1) * rows] = sine

    tiles(packed_rows, turn_rows)

    def put_operand(j, row, l, real, imag):
        for part, value in enumerate((real, imag)):
            parity, _ = place(j, row)
            high, low = split(value)
            columns = slice(part * lanes + l * rows, part * lanes + (l + 1) * rows)
            start = (j // 2) * packed_rows + row
            for copy_index, item in enumerate((high, low, high)):
                operand[parity, pl.ds(pl.multiple_of(copy_index * half + start, TILE), TILE), columns] = item

    def couple(target):
        for parity in range(2):
            target[1 - parity] = jnp.dot(
                table[parity], operand[parity], preferred_element_type=jnp.float32
            )

    def columns_of(part, l):
        return slice(part * lanes + l * rows, part * lanes + (l + 1) * rows)

    for n in range(1, tm_count - 1):
        hear_beside(entered_at(n))
        if n < tm_count - 2:
            tell_beside(entered_at(n + 1))
    for copy in line_copies[0]:
        copy.wait_recv()

    def field_rows(row):
        cosine, sine = cos_sin(lines[0, pl.ds(row, TILE)])
        lit = packed_mask[pl.ds(row, TILE)]
        wide_cos, wide_sin = widened(cosine * lit), widened(sine * lit)
        for j in range(pieces):
            parity, where = place(j, row)
            for l in range(groups):
                turn_cos = turn[0, j, pl.ds(row, TILE), l * rows : (l + 1) * rows]
                turn_sin = turn[1, j, pl.ds(row, TILE), l * rows : (l + 1) * rows]
                real = wide_cos[j] * turn_cos - wide_sin[j] * turn_sin
                imag = wide_cos[j] * turn_sin + wide_sin[j] * turn_cos
                field[parity, where, columns_of(0, l)] = real
                field[parity, where, columns_of(1, l)] = imag
                put_operand(j, row, l, real, imag)

    tiles(packed_rows, field_rows)
    copies[3].wait()
    couple(image)

    copies[2].wait()
    for copy, _, takes, _ in halos:
        pl.when(takes)(copy.wait_recv)
    before = pl.ds(
        pl.multiple_of(((mod + mod_count - 1) % mod_count) * width + (width - HALO), HALO), HALO
    )
    codes = jnp.concatenate(
        [wind[before], wind[pl.ds(pl.multiple_of(mod * width, HALO), width)]], axis=0
    )
    tall = HALO + width
    frac_x = ((codes & 3).astype(jnp.float32) + 0.5) * 0.25
    frac_r = ((codes >> 2).astype(jnp.float32) + 0.5) * 0.25
    stay_stay = (1.0 - frac_x) * (1.0 - frac_r)
    ahead_stay = frac_x * (1.0 - frac_r)
    stay_ahead = (1.0 - frac_x) * frac_r
    ahead_ahead = frac_x * frac_r
    lane = lax.broadcasted_iota(jnp.int32, (tall, rows), 1)
    pixel = mod * width - HALO + lax.broadcasted_iota(jnp.int32, (tall, rows), 0)
    total_frames = frames * tm_count
    flow_power = jnp.zeros((HALO, rows), jnp.float32)
    for i in range(frames + 1):
        base = extended[i, 0:tall]
        ahead = extended[i, 1 : tall + 1]
        crossing = stay_ahead * jnp.where(lane == rows - 1, 0.0, pltpu.roll(base, rows - 1, 1))
        crossing += ahead_ahead * jnp.where(lane == rows - 1, 0.0, pltpu.roll(ahead, rows - 1, 1))
        moved = stay_stay * base + ahead_stay * ahead + crossing
        flow_id = tm * frames - 1 + i
        valid = (pixel >= 0) & (flow_id >= 0) & (flow_id <= total_frames - 2)
        flow = jnp.where(valid, extended[i + 1, 0:tall] - moved, 0.0)
        if i >= 1:
            for start in range(HALO, tall, HALO):
                flow_power += flow[start : start + HALO] * flow[start : start + HALO]
            near[0] = ahead_stay * flow
            near[1] = ahead_ahead * flow
            behind = (stay_ahead * flow)[HALO:] + near[1, HALO - 1 : HALO - 1 + width]
            spread = (
                (stay_stay * flow)[HALO:]
                + near[0, HALO - 1 : HALO - 1 + width]
                + jnp.where(lane[HALO:] == 0, 0.0, pltpu.roll(behind, 1, 1))
            )
            prior[i - 1] = prior[i - 1] - spread
        if i < frames:
            prior[i] = flow[HALO:]

    for copy in line_copies[1]:
        copy.wait_recv()

    def dir_rows(row):
        wide = widened(lines[1, pl.ds(row, TILE)])
        for j in range(pieces):
            parity, where = place(j, row)
            dir_wide[parity, where] = wide[j]
            for l in range(groups):
                real = field[parity, where, columns_of(0, l)] * wide[j]
                imag = field[parity, where, columns_of(1, l)] * wide[j]
                put_operand(j, row, l, real, imag)

    tiles(packed_rows, dir_rows)
    couple(push)

    def signal_rows(i, power):
        row = pl.multiple_of(i * TILE, TILE)
        for j in range(pieces):
            parity, where = place(j, row)
            step = dir_wide[parity, where]
            even = odd = None
            for l in range(groups):
                er = field[parity, where, columns_of(0, l)]
                ei = field[parity, where, columns_of(1, l)]
                ur = image[parity, where, columns_of(0, l)]
                ui = image[parity, where, columns_of(1, l)]
                vr = push[parity, where, columns_of(0, l)]
                vi = push[parity, where, columns_of(1, l)]
                even_l = ui * vr - ur * vi
                odd_l = (ur * er + ui * ei) * step - (er * vr + ei * vi)
                even = even_l if even is None else even + even_l
                odd = odd_l if odd is None else odd + odd_l
            even = 2.0 * over_groups(even)
            odd = over_groups(odd)
            front = noise_wide[0, parity, where] * (even + odd)
            back = noise_wide[1, parity, where] * (even - odd)
            power = power + front * (even + odd) + back * (even - odd)
            both = front + back
            differ = 0.5 * (front - back)
            bent[parity, where] = differ
            for l in range(groups):
                er = field[parity, where, columns_of(0, l)]
                ei = field[parity, where, columns_of(1, l)]
                ur = image[parity, where, columns_of(0, l)]
                ui = image[parity, where, columns_of(1, l)]
                put_operand(j, row, l, differ * er - both * ui, differ * ei + both * ur)

        return power

    power = lax.fori_loop(
        0, packed_rows // TILE, signal_rows, jnp.zeros((TILE, rows), jnp.float32), unroll=2
    )
    parts_own = tm * mod_count + mod
    parts[parts_own] = (power[:HALO] + power[HALO:]) * (1.0 / pieces) + flow_power
    part_copies = []
    for slot, (a, b) in enumerate(peers):
        part_copies.append(
            pltpu.make_async_remote_copy(
                parts.at[parts_own],
                parts.at[parts_own],
                part_send.at[slot],
                part_recv.at[slot],
                device_id=peer(a, b),
                device_id_type=pl.DeviceIdType.MESH,
            )
        )
        part_copies[-1].start()
    def grad_rows(row):
        grad = []
        for j in range(pieces):
            parity, where = place(j, row)
            differ = bent[parity, where]
            acc = None
            for l in range(groups):
                er = field[parity, where, columns_of(0, l)]
                ei = field[parity, where, columns_of(1, l)]
                kr = differ * image[parity, where, columns_of(0, l)] + push[parity, where, columns_of(0, l)]
                ki = differ * image[parity, where, columns_of(1, l)] + push[parity, where, columns_of(1, l)]
                term = er * kr + ei * ki
                acc = term if acc is None else acc + term
            grad.append(2.0 * over_groups(acc))
        send_grad[pl.ds(row, TILE)] = at_lanes(grad)

    side_count, side_rows = mod_count // 2, packed_rows // 2
    own_side, own_place = mod // side_count, mod % side_count
    grad_copies = []
    for side, first in ((1 - own_side, 0), (own_side, 1)):
        start = pl.multiple_of(side * side_rows, TILE)
        for parity in range(2):
            for block in range(pieces // 2):
                some = pl.ds(pl.multiple_of(block * packed_rows + start, TILE), side_rows)
                push[1 - parity, some] = jnp.dot(
                    table[parity, some], operand[parity], preferred_element_type=jnp.float32
                )
        tiles(side_rows, lambda row: grad_rows(pl.multiple_of(start + row, TILE)))
        for n in range(first, side_count):
            place_there = (own_place + n) % side_count
            owner = side * side_count + place_there
            offset = (owner + mod_count - mod) % mod_count
            grad_copies.append(
                pltpu.make_async_remote_copy(
                    send_grad.at[pl.ds(pl.multiple_of(owner * sub, sub), sub)],
                    grads.at[mod],
                    grad_send.at[offset - 1],
                    grad_recv.at[offset - 1],
                    device_id={"tm": tm, "mod": owner},
                    device_id_type=pl.DeviceIdType.MESH,
                )
            )
            grad_copies[-1].start()
    grads[mod] = send_grad[my_lines]

    for copy in tilt_copies + line_copies[0] + line_copies[1]:
        copy.wait_send()
    for copy, sends, _, _ in halos:
        pl.when(sends)(copy.wait_send)
    for copy in grad_copies + part_copies:
        copy.wait()


def gather_kernel(entries, grads, prior, parts, out, curvature):
    frames, width, rows = prior.shape
    mod_count, sub, _ = grads.shape
    pieces = mod_count // frames
    chunk = rows // pieces
    lane_group = lax.broadcasted_iota(jnp.int32, (TILE, rows), 1) // chunk
    for f in range(frames):
        for base in range(0, sub, TILE):
            arrived = [grads[f * pieces + k, base : base + TILE] for k in range(pieces)]
            for j in range(pieces):
                where = pl.ds(base * pieces + j, TILE, stride=pieces)
                grad = None
                for k in range(pieces):
                    shift = (k - j) * chunk % rows
                    piece = pltpu.roll(arrived[k], shift, 1) if shift else arrived[k]
                    grad = piece if grad is None else jnp.where(lane_group == k, piece, grad)
                out[f, where, :] = grad + prior[f, where, :]
    whole = parts[0]
    for n in range(1, parts.shape[0]):
        whole = whole + parts[n]
    curvature[0] = jnp.sum(whole) / entries


def fused_device(phase, direction, pupil_mask, mod_tilts, wind_codes, noise_weight):
    frames, width, rows = phase.shape
    tm_count, mod_count = lax.axis_size("tm"), lax.axis_size("mod")
    pieces = mod_count // frames
    sub = width // pieces
    pupil = width * mod_count
    half = pupil // 2
    lanes = mod_count // pieces * rows
    packed_rows = pupil // pieces
    everyone = tm_count * mod_count
    vmem, smem, hbm = (
        pl.BlockSpec(memory_space=pltpu.VMEM),
        pl.BlockSpec(memory_space=pltpu.SMEM),
        pl.BlockSpec(memory_space=pl.ANY),
    )
    f32, bf16 = jnp.float32, jnp.bfloat16
    dma = pltpu.SemaphoreType.DMA
    sums = pl.pallas_call(
        functools.partial(fused_kernel, (tm_count, mod_count)),
        out_shape=(
            pltpu.VMEM((mod_count, sub, rows), f32),
            pltpu.VMEM(phase.shape, f32),
            pltpu.VMEM((everyone, HALO, rows), f32),
        ),
        in_specs=[hbm, hbm, vmem, hbm, hbm, hbm, hbm],
        out_specs=(vmem, vmem, vmem),
        scratch_shapes=[
            pltpu.VMEM((2, mod_count, sub, rows), f32),
            pltpu.VMEM((2, packed_rows, rows), f32),
            pltpu.VMEM((8, rows), f32),
            pltpu.VMEM((mod_count, 8, rows), f32),
            pltpu.VMEM((frames + 2, width + 2 * HALO, rows), f32),
            pltpu.VMEM(pupil_mask.shape, jnp.int32),
            pltpu.VMEM(wind_codes.shape, jnp.int32),
            pltpu.VMEM(noise_weight.shape[1:], f32),
            pltpu.VMEM((2, half, 3 * half), bf16),
            pltpu.VMEM((packed_rows, rows), f32),
            pltpu.VMEM((2, 2, half, rows), f32),
            pltpu.VMEM((2, pieces, packed_rows, lanes), f32),
            pltpu.VMEM((2, half, 2 * lanes), f32),
            pltpu.VMEM((2, 3 * half, 2 * lanes), bf16),
            pltpu.VMEM((2, half, 2 * lanes), f32),
            pltpu.VMEM((2, half, 2 * lanes), f32),
            pltpu.VMEM((2, half, rows), f32),
            pltpu.VMEM((2, half, rows), f32),
            pltpu.VMEM((2, width + HALO, rows), f32),
            pltpu.VMEM((packed_rows, rows), f32),
            pltpu.VMEM(phase.shape, f32),
            pltpu.VMEM(direction.shape, f32),
            dma((6,)),
            dma((3, mod_count - 1)),
            dma((3, mod_count - 1)),
            dma((8,)),
            dma((8,)),
            dma((mod_count - 1,)),
            dma((mod_count - 1,)),
            dma((everyone - 1,)),
            dma((everyone - 1,)),
            pltpu.SemaphoreType.REGULAR((max(tm_count - 1, 1), 2)),
        ],
        compiler_params=pltpu.CompilerParams(collective_id=0, has_side_effects=True),
    )(
        phase,
        direction,
        mod_tilts.reshape(1, 1),
        pupil_mask,
        wind_codes,
        noise_weight,
        jnp.asarray(coupling_tables(pupil, pieces)),
    )
    return pl.pallas_call(
        functools.partial(gather_kernel, float(frames * tm_count * pupil * rows)),
        out_shape=(jax.ShapeDtypeStruct(phase.shape, f32), jax.ShapeDtypeStruct((1,), f32)),
        in_specs=[vmem, vmem, vmem],
        out_specs=(vmem, smem),
    )(*[pltpu.with_memory_space_constraint(item, pltpu.VMEM) for item in sums])


def device_program(phase, direction, pupil_mask, mod_tilts, wind_codes, noise_weight):
    frames, width, rows = phase.shape
    mod_count = lax.axis_size("mod")
    fits = mod_count % frames == 0 and mod_tilts.shape[0] == 1 and frames > 1
    if fits:
        pieces = mod_count // frames
        fits = (
            lax.axis_size("tm") > 1
            and pieces % 2 == 0
            and rows == 128
            and rows % pieces == 0
            and width % (pieces * TILE) == 0
            and mod_count % 2 == 0
            and pieces & (pieces - 1) == 0
        )
    run = fused_device if fits else per_device
    return run(phase, direction, pupil_mask, mod_tilts, wind_codes, noise_weight)


def solution(mesh):
    return jax.shard_map(
        device_program,
        mesh=mesh,
        in_specs=(
            P(("grp", "tm"), "mod", None),
            P(("grp", "tm"), "mod", None),
            P(),
            P("mod"),
            P("grp", None),
            P(("grp", "tm"), None, None),
        ),
        out_specs=(P(("grp", "tm"), "mod", None), P("grp")),
        check_vma=False,
    )
```

```python
import functools

import jax
import jax.numpy as jnp
import numpy as np
from jax import lax
from jax.experimental import pallas as pl
from jax.experimental.pallas import tpu as pltpu
from jax.sharding import PartitionSpec as P

HIGHEST = lax.Precision.HIGHEST


def with_halo(cells, sides, width):
    for axis, dim in sides:
        count = lax.axis_size(axis)
        ends = count - 1
        head = lax.slice_in_dim(cells, 0, width, axis=dim)
        tail = lax.slice_in_dim(cells, cells.shape[dim] - width, cells.shape[dim], axis=dim)
        cells = jnp.concatenate(
            [
                lax.ppermute(tail, axis, [(i, (i + 1) % count) for i in range(ends)]),
                cells,
                lax.ppermute(head, axis, [((i + 1) % count, i) for i in range(ends)]),
            ],
            axis=dim,
        )
    return cells


def square_table(count, orient):
    index_range = jnp.arange(count, dtype=jnp.int32)
    turn_counts = index_range[:, None] * index_range[None, :] % count
    angles = orient * 2.0 * jnp.pi / count * turn_counts.astype(jnp.float32)
    return (jnp.cos(angles), jnp.sin(angles))


def complex_mix(form, table_real, table_imag, field_real, field_imag):
    real_real = jnp.einsum(form, table_real, field_real, precision=HIGHEST)
    imag_imag = jnp.einsum(form, table_imag, field_imag, precision=HIGHEST)
    real_imag = jnp.einsum(form, table_real, field_imag, precision=HIGHEST)
    imag_real = jnp.einsum(form, table_imag, field_real, precision=HIGHEST)
    return (real_real - imag_imag, real_imag + imag_real)


def transform(field_real, field_imag, orient):
    batch_size, length, row_count = field_real.shape
    outer_size = 32
    inner_size = length // outer_size
    first_real, first_imag = square_table(outer_size, orient)
    second_real, second_imag = square_table(inner_size, orient)
    turn_counts = (
        jnp.arange(outer_size, dtype=jnp.int32)[:, None]
        * jnp.arange(inner_size, dtype=jnp.int32)[None, :]
        % length
    )
    angles = orient * 2.0 * jnp.pi / length * turn_counts.astype(jnp.float32)
    twist_real = jnp.cos(angles)[None, :, :, None]
    twist_imag = jnp.sin(angles)[None, :, :, None]
    shaped_real = field_real.reshape(batch_size, outer_size, inner_size, row_count)
    shaped_imag = field_imag.reshape(batch_size, outer_size, inner_size, row_count)
    section_real, section_imag = complex_mix(
        "kn,bnmr->bkmr", first_real, first_imag, shaped_real, shaped_imag
    )
    turned_real = section_real * twist_real - section_imag * twist_imag
    turned_imag = section_real * twist_imag + section_imag * twist_real
    final_real, final_imag = complex_mix(
        "dm,bkmr->bdkr", second_real, second_imag, turned_real, turned_imag
    )
    return (
        final_real.reshape(batch_size, length, row_count),
        final_imag.reshape(batch_size, length, row_count),
    )


def roof_mask(length, shift_bins):
    freq_index = jnp.arange(length, dtype=jnp.int32)
    signed_freq = jnp.where(freq_index < length // 2, freq_index, freq_index - length)
    turn_counts = shift_bins * jnp.abs(signed_freq) % length
    angles = -2.0 * jnp.pi / length * turn_counts.astype(jnp.float32)
    return (jnp.cos(angles), jnp.sin(angles))


def pyramid(field_real, field_imag, gain_real, gain_imag):
    spectrum_real, spectrum_imag = transform(field_real, field_imag, -1.0)
    column_real = gain_real[None, :, None]
    column_imag = gain_imag[None, :, None]
    masked_real = spectrum_real * column_real - spectrum_imag * column_imag
    masked_imag = spectrum_real * column_imag + spectrum_imag * column_real
    back_real, back_imag = transform(masked_real, masked_imag, 1.0)
    inverse_length = 1.0 / field_real.shape[1]
    return (back_real * inverse_length, back_imag * inverse_length)


def row_ahead(field):
    return jnp.pad(field[:, :, 1:], ((0, 0), (0, 0), (0, 1)))


def row_behind(field):
    return jnp.pad(field[:, :, :-1], ((0, 0), (0, 0), (1, 0)))


def flow_terms(extended, frac_x, frac_r, first_frame, total_frames, first_pixel):
    frames_ext, width_ext, row_count = extended.shape
    frames_dev = frames_ext - 2
    near_x = jnp.pad(frac_x, ((1, 0), (0, 0)))
    near_r = jnp.pad(frac_r, ((1, 0), (0, 0)))
    stay_stay = (1.0 - near_x) * (1.0 - near_r)
    ahead_stay = near_x * (1.0 - near_r)
    stay_ahead = (1.0 - near_x) * near_r
    ahead_ahead = near_x * near_r
    base_cells = extended[:, :-1, :]
    ahead_cells = extended[:, 1:, :]
    moved = (
        stay_stay * base_cells
        + ahead_stay * ahead_cells
        + stay_ahead * row_ahead(base_cells)
        + ahead_ahead * row_ahead(ahead_cells)
    )
    flow = extended[1:, :-1, :] - moved[:-1]
    frame_ids = first_frame - 1 + lax.broadcasted_iota(jnp.int32, flow.shape, 0)
    pixel_ids = first_pixel - 1 + lax.broadcasted_iota(jnp.int32, flow.shape, 1)
    valid = (frame_ids >= 0) & (frame_ids <= total_frames - 2) & (pixel_ids >= 0)
    flow = jnp.where(valid, flow, 0.0)
    spread = (
        (stay_stay * flow)[:, 1:]
        + (ahead_stay * flow)[:, :-1]
        + row_behind((stay_ahead * flow)[:, 1:] + (ahead_ahead * flow)[:, :-1])
    )
    prior = flow[:frames_dev, 1:] - spread[1:]
    return (prior, flow[1:, 1:])


def forward_pass(full_phase, full_direction, tilts, amplitude, gain_real, gain_imag):
    frames_dev, pupil_width, row_count = full_phase.shape
    line_length = 2 * pupil_width
    quarter = pupil_width // 2
    local_points = tilts.shape[0]
    positions = quarter + jnp.arange(pupil_width, dtype=jnp.int32)
    tilt_turns = tilts[:, None] * positions[None, :] % line_length
    tilt_angles = 2.0 * jnp.pi / line_length * tilt_turns.astype(jnp.float32)
    angles = full_phase[None] + tilt_angles[:, None, :, None]
    field_real = amplitude * jnp.cos(angles)
    field_imag = amplitude * jnp.sin(angles)
    margins = ((0, 0), (quarter, quarter), (0, 0))
    line_batch = local_points * frames_dev

    def padded_lines(field):
        return jnp.pad(field.reshape(line_batch, pupil_width, row_count), margins)

    image_real, image_imag = pyramid(
        padded_lines(field_real), padded_lines(field_imag), gain_real, gain_imag
    )
    push_real, push_imag = pyramid(
        padded_lines(-field_imag * full_direction),
        padded_lines(field_real * full_direction),
        gain_real,
        gain_imag,
    )
    signal_terms = (2.0 * (image_real * push_real + image_imag * push_imag)).reshape(
        local_points, frames_dev, line_length, row_count
    )
    return (field_real, field_imag, image_real, image_imag, jnp.sum(signal_terms, axis=0))


def backward_pass(
    field_real, field_imag, image_real, image_imag, weighted_full, gain_real, gain_imag
):
    local_points, frames_dev, pupil_width, row_count = field_real.shape
    line_length = 2 * pupil_width
    quarter = pupil_width // 2
    line_batch = local_points * frames_dev
    image_shaped_real = image_real.reshape(local_points, frames_dev, line_length, row_count)
    image_shaped_imag = image_imag.reshape(local_points, frames_dev, line_length, row_count)
    source_real = (weighted_full[None] * image_shaped_real).reshape(
        line_batch, line_length, row_count
    )
    source_imag = (weighted_full[None] * image_shaped_imag).reshape(
        line_batch, line_length, row_count
    )
    back_real, back_imag = pyramid(source_real, source_imag, gain_real, -gain_imag)
    back_real = back_real[:, quarter : quarter + pupil_width].reshape(
        local_points, frames_dev, pupil_width, row_count
    )
    back_imag = back_imag[:, quarter : quarter + pupil_width].reshape(
        local_points, frames_dev, pupil_width, row_count
    )
    return -2.0 * jnp.sum(field_imag * back_real - field_real * back_imag, axis=0)


def per_device(phase, direction, pupil_mask, mod_tilts, wind_codes, noise_weight):
    frames_dev, shard_width, row_count = phase.shape
    mod_count = lax.axis_size("mod")
    pupil_width = shard_width * mod_count
    line_length = 2 * pupil_width
    quarter = pupil_width // 2
    mod_index = lax.axis_index("mod")
    first_frame = lax.axis_index("tm") * frames_dev
    total_frames = frames_dev * lax.axis_size("tm")
    first_pixel = mod_index * shard_width
    frac_x = ((wind_codes % 4).astype(jnp.float32) + 0.5) / 4.0
    frac_r = ((wind_codes // 4).astype(jnp.float32) + 0.5) / 4.0
    gain_real, gain_imag = roof_mask(line_length, quarter)
    rimmed = with_halo(direction, (("tm", 0),), 1)
    full_phase, full_rim = (
        lax.all_gather(phase, "mod", axis=1, tiled=True),
        lax.all_gather(rimmed, "mod", axis=1, tiled=True),
    )
    full_direction = full_rim[1:-1]
    extended = jnp.pad(full_rim, ((0, 0), (1, 1), (0, 0)))
    prior_lines, flow_lines = flow_terms(extended, frac_x, frac_r, first_frame, total_frames, 0)
    prior = lax.dynamic_slice_in_dim(prior_lines, first_pixel, shard_width, 1)
    amplitude = pupil_mask.astype(jnp.float32)
    field_real, field_imag, image_real, image_imag, signal_local = forward_pass(
        full_phase, full_direction, mod_tilts, amplitude, gain_real, gain_imag
    )
    signal_full = lax.psum(signal_local, "mod")
    weighted_used = noise_weight * signal_full
    grad_lines = backward_pass(
        field_real, field_imag, image_real, image_imag, weighted_used, gain_real, gain_imag
    )
    grad_own = lax.psum_scatter(grad_lines, "mod", scatter_dimension=1, tiled=True)
    hess_vec = grad_own + prior
    curvature_total = lax.psum(jnp.sum(direction * hess_vec), ("tm", "mod"))
    entry_count = float(total_frames * pupil_width * row_count)
    curvature = (curvature_total / entry_count).reshape(1)
    return (hess_vec, curvature)


TILE = 16
HALO = 8


def coupling_tables(pupil_width, pieces):
    per_piece = pupil_width // pieces
    order = [
        np.concatenate([pieces * np.arange(per_piece) + j for j in range(parity, pieces, 2)])
        for parity in (0, 1)
    ]
    tables = []
    for source in (0, 1):
        gap = order[1 - source][:, None] - order[source][None, :]
        exact = -1.0 / (pupil_width * np.sin(np.pi * gap / pupil_width))
        high = exact.astype(jnp.bfloat16)
        low = (exact - high.astype(np.float64)).astype(jnp.bfloat16)
        tables.append(np.concatenate([high, high, low], axis=1))
    return np.stack(tables)


def cos_sin(angle):
    turns = jnp.round(angle * np.float32(2.0 / np.pi))
    rest = angle - turns * np.float32(1.5703125)
    rest = rest - turns * np.float32(4.837512969970703125e-4)
    rest = rest - turns * np.float32(7.54978995489188216e-8)
    square = rest * rest
    sine = rest + rest * square * (
        np.float32(-1.6666654611e-1)
        + square * (np.float32(8.3321608736e-3) + square * np.float32(-1.9515295891e-4))
    )
    cosine = (
        1.0
        - 0.5 * square
        + square
        * square
        * (
            np.float32(4.166664568298827e-2)
            + square * (np.float32(-1.388731625493765e-3) + square * np.float32(2.443315711809948e-5))
        )
    )
    quarter = turns.astype(jnp.int32)
    swap = (quarter & 1) == 1
    out_cos = jnp.where(swap, sine, cosine)
    out_sin = jnp.where(swap, cosine, sine)
    out_cos = jnp.where(((quarter + 1) & 2) == 2, -out_cos, out_cos)
    out_sin = jnp.where((quarter & 2) == 2, -out_sin, out_sin)
    return out_cos, out_sin


def split(value):
    high = value.astype(jnp.bfloat16)
    return high, (value - high.astype(jnp.float32)).astype(jnp.bfloat16)


def fused_kernel(
    counts,
    phase_hbm,
    direction_hbm,
    tilts,
    mask_hbm,
    wind_hbm,
    noise_hbm,
    table_hbm,
    grads,
    prior,
    parts,
    send_lines,
    lines,
    send_tilt,
    tilt_tiles,
    extended,
    mask,
    wind,
    noise,
    table,
    packed_mask,
    noise_wide,
    turn,
    field,
    operand,
    image,
    push,
    dir_wide,
    bent,
    near,
    send_grad,
    phase,
    direction,
    local_sem,
    line_send,
    line_recv,
    halo_send,
    halo_recv,
    grad_send,
    grad_recv,
    part_send,
    part_recv,
    entered,
):
    tm_count, mod_count = counts
    frames, width, rows = phase.shape
    chunks = mod_count // frames
    chunk = rows // chunks
    pieces = chunks
    sub = width // pieces
    pupil = width * mod_count
    length = 2 * pupil
    packed_rows = pupil // pieces
    half = pupil // 2
    groups = mod_count // pieces
    lanes = groups * rows
    tm = lax.axis_index("tm")
    mod = lax.axis_index("mod")
    own_frame = mod // chunks
    own_chunk = mod % chunks

    copies = [
        pltpu.make_async_copy(noise_hbm.at[own_frame], noise, local_sem.at[0]),
        pltpu.make_async_copy(mask_hbm, mask, local_sem.at[1]),
        pltpu.make_async_copy(wind_hbm, wind, local_sem.at[2]),
        pltpu.make_async_copy(table_hbm, table, local_sem.at[3]),
        pltpu.make_async_copy(phase_hbm, phase, local_sem.at[4]),
        pltpu.make_async_copy(direction_hbm, direction, local_sem.at[5]),
    ]

    barrier = pltpu.get_barrier_semaphore()
    peers = [
        (a, b) for a in range(tm_count) for b in range(mod_count) if (a, b) != (0, 0)
    ]

    def peer(a, b):
        return {"tm": (tm + a) % tm_count, "mod": (mod + b) % mod_count}

    for b in range(1, mod_count):
        pl.semaphore_signal(
            barrier, inc=1, device_id=peer(0, b), device_id_type=pl.DeviceIdType.MESH
        )
    beside = [(-1, tm > 0), (1, tm < tm_count - 1)]

    def tell_beside(semaphores):
        for side, (step, exists) in enumerate(beside):

            @pl.when(exists)
            def _():
                pl.semaphore_signal(
                    semaphores[1 - side],
                    inc=1,
                    device_id=peer(step, 0),
                    device_id_type=pl.DeviceIdType.MESH,
                )

    def hear_beside(semaphores):
        for side, (step, exists) in enumerate(beside):

            @pl.when(exists)
            def _():
                pl.semaphore_wait(semaphores[side], 1)

    def entered_at(n):
        return [entered.at[n, 0], entered.at[n, 1]]

    tell_beside([barrier, barrier])
    for copy in copies[4:] + copies[:4]:
        copy.start()

    lane_group = lax.broadcasted_iota(jnp.int32, (TILE, rows), 1) // chunk

    def at_lanes(values):
        out_value = values[0]
        for j in range(1, len(values)):
            out_value = jnp.where(lane_group[: out_value.shape[0]] == j, values[j], out_value)
        return out_value

    def turned(value, amount):
        if isinstance(amount, int):
            amount = amount % rows
            if amount == 0:
                return value
        return pltpu.roll(value, amount, 1)

    def widened(value):
        shifts = [turned(value, s * chunk) for s in range(pieces)]
        return [
            at_lanes([shifts[(m - j) % pieces] for m in range(pieces)]) for j in range(pieces)
        ]

    def over_groups(value):
        step = chunk
        while step < rows:
            value = value + pltpu.roll(value, step, 1)
            step *= 2
        return value

    def tiles(n, body, unroll=2):
        def step(i, carry):
            body(pl.multiple_of(i * TILE, TILE))
            return carry

        lax.fori_loop(0, n // TILE, step, 0, unroll=unroll)

    for which, source in enumerate((phase, direction)):
        copies[4 + which].wait()
        for f in range(frames):
            for base in range(0, sub, TILE):
                loaded = [
                    source[f, pl.ds(base * pieces + j, TILE, stride=pieces), :]
                    for j in range(pieces)
                ]
                for k in range(chunks):
                    send_lines[which, f * chunks + k, base : base + TILE] = at_lanes(
                        [turned(loaded[j], (j - k) * chunk) for j in range(pieces)]
                    )

    send_tilt[...] = jnp.broadcast_to(tilts[...].astype(jnp.float32), send_tilt.shape)
    earlier, later = (tm + tm_count - 1) // tm_count, (2 * tm_count - 2 - tm) // tm_count
    pl.semaphore_wait(barrier, mod_count - 1 + earlier + later)

    my_lines = pl.ds(pl.multiple_of(mod * sub, sub), sub)
    tilt_copies, line_copies = [], [[], []]
    for o in range(1, mod_count):
        tilt_copies.append(
            pltpu.make_async_remote_copy(
                send_tilt,
                tilt_tiles.at[mod],
                line_send.at[2, o - 1],
                line_recv.at[2, o - 1],
                device_id=peer(0, o),
                device_id_type=pl.DeviceIdType.MESH,
            )
        )
        for which in range(2):
            line_copies[which].append(
                pltpu.make_async_remote_copy(
                    send_lines.at[which, (mod + o) % mod_count],
                    lines.at[which, my_lines],
                    line_send.at[which, o - 1],
                    line_recv.at[which, o - 1],
                    device_id=peer(0, o),
                    device_id_type=pl.DeviceIdType.MESH,
                )
            )
    for copy in tilt_copies + line_copies[0]:
        copy.start()
    tell_beside(entered_at(0))

    halos, corners = [], []
    for da in (-1, 0, 1):
        for db in (-1, 0, 1):
            if (da, db) == (0, 0):
                continue
            src_f, dst_f, n_f = {1: (frames - 1, 0, 1), 0: (0, 1, frames), -1: (0, frames + 1, 1)}[da]
            src_x, dst_x, n_x = {
                1: (width - HALO, 0, HALO),
                0: (0, HALO, width),
                -1: (0, HALO + width, HALO),
            }[db]
            slot = len(halos)
            copy = pltpu.make_async_remote_copy(
                direction.at[pl.ds(src_f, n_f), pl.ds(src_x, n_x)],
                extended.at[pl.ds(dst_f, n_f), pl.ds(dst_x, n_x)],
                halo_send.at[slot],
                halo_recv.at[slot],
                device_id=peer(da, db),
                device_id_type=pl.DeviceIdType.MESH,
            )
            sends = (tm + da >= 0) & (tm + da < tm_count) & (mod + db >= 0) & (mod + db < mod_count)
            takes = (tm - da >= 0) & (tm - da < tm_count) & (mod - db >= 0) & (mod - db < mod_count)
            halos.append((copy, sends, takes, (dst_f, n_f, dst_x, n_x)))
            if da == 0 or db == 0:
                pl.when(sends)(copy.start)
            else:
                corners.append((copy, sends))
    for copy in line_copies[1]:
        copy.start()

    for which in range(2):
        lines[which, my_lines] = send_lines[which, mod]
    tilt_tiles[mod] = send_tilt[...]
    extended[1 : 1 + frames, HALO : HALO + width] = direction[...]
    for _, _, takes, (dst_f, n_f, dst_x, n_x) in halos:

        @pl.when(jnp.logical_not(takes))
        def _():
            extended[dst_f : dst_f + n_f, dst_x : dst_x + n_x] = jnp.zeros(
                (n_f, n_x, rows), jnp.float32
            )

    copies[1].wait()
    copies[0].wait()

    def pack_own(source, base, row):
        return at_lanes(
            [
                pltpu.roll(
                    source[pl.ds(base + row * pieces + j, TILE, stride=pieces), :],
                    ((j + chunks - own_chunk) % chunks) * chunk,
                    1,
                )
                for j in range(pieces)
            ]
        )

    def place(j, row):
        return j % 2, pl.ds(pl.multiple_of((j // 2) * packed_rows + row, TILE), TILE)

    def pack_rows(row):
        packed_mask[pl.ds(row, TILE)] = pack_own(mask, 0, row).astype(jnp.float32)
        for side in range(2):
            wide = widened(pack_own(noise, side * pupil, row))
            for j in range(pieces):
                parity, where = place(j, row)
                noise_wide[side, parity, where] = wide[j]

    tiles(packed_rows, pack_rows)

    hear_beside(entered_at(0))
    for copy, sends in corners:
        pl.when(sends)(copy.start)
    if tm_count > 2:
        tell_beside(entered_at(1))
    for copy in tilt_copies:
        copy.wait_recv()

    def turn_rows(row):
        for l in range(groups):
            tilt = at_lanes([tilt_tiles[l * pieces + m] for m in range(pieces)]).astype(jnp.int32)
            tilt = jnp.concatenate([tilt] * (TILE // tilt.shape[0]), axis=0)
            index = row + lax.broadcasted_iota(jnp.int32, (TILE, rows), 0)
            for j in range(pieces):
                position = half + pieces * index + j
                product = tilt * position
                if length & (length - 1) == 0:
                    product = product & (length - 1)
                else:
                    product = product % length
                cosine, sine = cos_sin(
                    np.float32(2.0 * np.pi / length) * product.astype(jnp.float32)
                )
                turn[0, j, pl.ds(row, TILE), l * rows : (l + 1) * rows] = cosine
                turn[1, j, pl.ds(row, TILE), l * rows : (l + 1) * rows] = sine

    tiles(packed_rows, turn_rows)

    def put_operand(j, row, l, real, imag):
        for part, value in enumerate((real, imag)):
            parity, _ = place(j, row)
            high, low = split(value)
            columns = slice(part * lanes + l * rows, part * lanes + (l + 1) * rows)
            start = (j // 2) * packed_rows + row
            for copy_index, item in enumerate((high, low, high)):
                operand[parity, pl.ds(pl.multiple_of(copy_index * half + start, TILE), TILE), columns] = item

    def couple(target):
        for parity in range(2):
            target[1 - parity] = jnp.dot(
                table[parity], operand[parity], preferred_element_type=jnp.float32
            )

    def columns_of(part, l):
        return slice(part * lanes + l * rows, part * lanes + (l + 1) * rows)

    for n in range(1, tm_count - 1):
        hear_beside(entered_at(n))
        if n < tm_count - 2:
            tell_beside(entered_at(n + 1))
    for copy in line_copies[0]:
        copy.wait_recv()

    def field_rows(row):
        cosine, sine = cos_sin(lines[0, pl.ds(row, TILE)])
        lit = packed_mask[pl.ds(row, TILE)]
        wide_cos, wide_sin = widened(cosine * lit), widened(sine * lit)
        for j in range(pieces):
            parity, where = place(j, row)
            for l in range(groups):
                turn_cos = turn[0, j, pl.ds(row, TILE), l * rows : (l + 1) * rows]
                turn_sin = turn[1, j, pl.ds(row, TILE), l * rows : (l + 1) * rows]
                real = wide_cos[j] * turn_cos - wide_sin[j] * turn_sin
                imag = wide_cos[j] * turn_sin + wide_sin[j] * turn_cos
                field[parity, where, columns_of(0, l)] = real
                field[parity, where, columns_of(1, l)] = imag
                put_operand(j, row, l, real, imag)

    tiles(packed_rows, field_rows)
    copies[3].wait()
    couple(image)

    copies[2].wait()
    for copy, _, takes, _ in halos:
        pl.when(takes)(copy.wait_recv)
    before = pl.ds(
        pl.multiple_of(((mod + mod_count - 1) % mod_count) * width + (width - HALO), HALO), HALO
    )
    codes = jnp.concatenate(
        [wind[before], wind[pl.ds(pl.multiple_of(mod * width, HALO), width)]], axis=0
    )
    tall = HALO + width
    frac_x = ((codes & 3).astype(jnp.float32) + 0.5) * 0.25
    frac_r = ((codes >> 2).astype(jnp.float32) + 0.5) * 0.25
    stay_stay = (1.0 - frac_x) * (1.0 - frac_r)
    ahead_stay = frac_x * (1.0 - frac_r)
    stay_ahead = (1.0 - frac_x) * frac_r
    ahead_ahead = frac_x * frac_r
    lane = lax.broadcasted_iota(jnp.int32, (tall, rows), 1)
    pixel = mod * width - HALO + lax.broadcasted_iota(jnp.int32, (tall, rows), 0)
    total_frames = frames * tm_count
    flow_power = jnp.zeros((HALO, rows), jnp.float32)
    for i in range(frames + 1):
        base = extended[i, 0:tall]
        ahead = extended[i, 1 : tall + 1]
        crossing = stay_ahead * jnp.where(lane == rows - 1, 0.0, pltpu.roll(base, rows - 1, 1))
        crossing += ahead_ahead * jnp.where(lane == rows - 1, 0.0, pltpu.roll(ahead, rows - 1, 1))
        moved = stay_stay * base + ahead_stay * ahead + crossing
        flow_id = tm * frames - 1 + i
        valid = (pixel >= 0) & (flow_id >= 0) & (flow_id <= total_frames - 2)
        flow = jnp.where(valid, extended[i + 1, 0:tall] - moved, 0.0)
        if i >= 1:
            for start in range(HALO, tall, HALO):
                flow_power += flow[start : start + HALO] * flow[start : start + HALO]
            near[0] = ahead_stay * flow
            near[1] = ahead_ahead * flow
            behind = (stay_ahead * flow)[HALO:] + near[1, HALO - 1 : HALO - 1 + width]
            spread = (
                (stay_stay * flow)[HALO:]
                + near[0, HALO - 1 : HALO - 1 + width]
                + jnp.where(lane[HALO:] == 0, 0.0, pltpu.roll(behind, 1, 1))
            )
            prior[i - 1] = prior[i - 1] - spread
        if i < frames:
            prior[i] = flow[HALO:]

    for copy in line_copies[1]:
        copy.wait_recv()

    def dir_rows(row):
        wide = widened(lines[1, pl.ds(row, TILE)])
        for j in range(pieces):
            parity, where = place(j, row)
            dir_wide[parity, where] = wide[j]
            for l in range(groups):
                real = field[parity, where, columns_of(0, l)] * wide[j]
                imag = field[parity, where, columns_of(1, l)] * wide[j]
                put_operand(j, row, l, real, imag)

    tiles(packed_rows, dir_rows)
    couple(push)

    def signal_rows(i, power):
        row = pl.multiple_of(i * TILE, TILE)
        for j in range(pieces):
            parity, where = place(j, row)
            step = dir_wide[parity, where]
            even = odd = None
            for l in range(groups):
                er = field[parity, where, columns_of(0, l)]
                ei = field[parity, where, columns_of(1, l)]
                ur = image[parity, where, columns_of(0, l)]
                ui = image[parity, where, columns_of(1, l)]
                vr = push[parity, where, columns_of(0, l)]
                vi = push[parity, where, columns_of(1, l)]
                even_l = ui * vr - ur * vi
                odd_l = (ur * er + ui * ei) * step - (er * vr + ei * vi)
                even = even_l if even is None else even + even_l
                odd = odd_l if odd is None else odd + odd_l
            even = 2.0 * over_groups(even)
            odd = over_groups(odd)
            front = noise_wide[0, parity, where] * (even + odd)
            back = noise_wide[1, parity, where] * (even - odd)
            power = power + front * (even + odd) + back * (even - odd)
            both = front + back
            differ = 0.5 * (front - back)
            bent[parity, where] = differ
            for l in range(groups):
                er = field[parity, where, columns_of(0, l)]
                ei = field[parity, where, columns_of(1, l)]
                ur = image[parity, where, columns_of(0, l)]
                ui = image[parity, where, columns_of(1, l)]
                put_operand(j, row, l, differ * er - both * ui, differ * ei + both * ur)

        return power

    power = lax.fori_loop(
        0, packed_rows // TILE, signal_rows, jnp.zeros((TILE, rows), jnp.float32), unroll=2
    )
    parts_own = tm * mod_count + mod
    parts[parts_own] = (power[:HALO] + power[HALO:]) * (1.0 / pieces) + flow_power
    part_copies = []
    for slot, (a, b) in enumerate(peers):
        part_copies.append(
            pltpu.make_async_remote_copy(
                parts.at[parts_own],
                parts.at[parts_own],
                part_send.at[slot],
                part_recv.at[slot],
                device_id=peer(a, b),
                device_id_type=pl.DeviceIdType.MESH,
            )
        )
        part_copies[-1].start()
    couple(push)

    def grad_rows(row):
        grad = []
        for j in range(pieces):
            parity, where = place(j, row)
            differ = bent[parity, where]
            acc = None
            for l in range(groups):
                er = field[parity, where, columns_of(0, l)]
                ei = field[parity, where, columns_of(1, l)]
                kr = differ * image[parity, where, columns_of(0, l)] + push[parity, where, columns_of(0, l)]
                ki = differ * image[parity, where, columns_of(1, l)] + push[parity, where, columns_of(1, l)]
                term = er * kr + ei * ki
                acc = term if acc is None else acc + term
            grad.append(2.0 * over_groups(acc))
        send_grad[pl.ds(row, TILE)] = at_lanes(grad)

    tiles(packed_rows, grad_rows)

    grad_copies = []
    for o in range(1, mod_count):
        owner = (mod + o) % mod_count
        grad_copies.append(
            pltpu.make_async_remote_copy(
                send_grad.at[pl.ds(pl.multiple_of(owner * sub, sub), sub)],
                grads.at[mod],
                grad_send.at[o - 1],
                grad_recv.at[o - 1],
                device_id=peer(0, o),
                device_id_type=pl.DeviceIdType.MESH,
            )
        )
        grad_copies[-1].start()
    grads[mod] = send_grad[my_lines]

    for copy in tilt_copies + line_copies[0] + line_copies[1]:
        copy.wait_send()
    for copy, sends, _, _ in halos:
        pl.when(sends)(copy.wait_send)
    for copy in grad_copies + part_copies:
        copy.wait()


def gather_kernel(entries, grads, prior, parts, out, curvature):
    frames, width, rows = prior.shape
    mod_count, sub, _ = grads.shape
    pieces = mod_count // frames
    chunk = rows // pieces
    lane_group = lax.broadcasted_iota(jnp.int32, (TILE, rows), 1) // chunk
    for f in range(frames):
        for base in range(0, sub, TILE):
            arrived = [grads[f * pieces + k, base : base + TILE] for k in range(pieces)]
            for j in range(pieces):
                where = pl.ds(base * pieces + j, TILE, stride=pieces)
                grad = None
                for k in range(pieces):
                    shift = (k - j) * chunk % rows
                    piece = pltpu.roll(arrived[k], shift, 1) if shift else arrived[k]
                    grad = piece if grad is None else jnp.where(lane_group == k, piece, grad)
                out[f, where, :] = grad + prior[f, where, :]
    whole = parts[0]
    for n in range(1, parts.shape[0]):
        whole = whole + parts[n]
    curvature[0] = jnp.sum(whole) / entries


def fused_device(phase, direction, pupil_mask, mod_tilts, wind_codes, noise_weight):
    frames, width, rows = phase.shape
    tm_count, mod_count = lax.axis_size("tm"), lax.axis_size("mod")
    pieces = mod_count // frames
    sub = width // pieces
    pupil = width * mod_count
    half = pupil // 2
    lanes = mod_count // pieces * rows
    packed_rows = pupil // pieces
    everyone = tm_count * mod_count
    vmem, smem, hbm = (
        pl.BlockSpec(memory_space=pltpu.VMEM),
        pl.BlockSpec(memory_space=pltpu.SMEM),
        pl.BlockSpec(memory_space=pl.ANY),
    )
    f32, bf16 = jnp.float32, jnp.bfloat16
    dma = pltpu.SemaphoreType.DMA
    sums = pl.pallas_call(
        functools.partial(fused_kernel, (tm_count, mod_count)),
        out_shape=(
            pltpu.VMEM((mod_count, sub, rows), f32),
            pltpu.VMEM(phase.shape, f32),
            pltpu.VMEM((everyone, HALO, rows), f32),
        ),
        in_specs=[hbm, hbm, vmem, hbm, hbm, hbm, hbm],
        out_specs=(vmem, vmem, vmem),
        scratch_shapes=[
            pltpu.VMEM((2, mod_count, sub, rows), f32),
            pltpu.VMEM((2, packed_rows, rows), f32),
            pltpu.VMEM((8, rows), f32),
            pltpu.VMEM((mod_count, 8, rows), f32),
            pltpu.VMEM((frames + 2, width + 2 * HALO, rows), f32),
            pltpu.VMEM(pupil_mask.shape, jnp.int32),
            pltpu.VMEM(wind_codes.shape, jnp.int32),
            pltpu.VMEM(noise_weight.shape[1:], f32),
            pltpu.VMEM((2, half, 3 * half), bf16),
            pltpu.VMEM((packed_rows, rows), f32),
            pltpu.VMEM((2, 2, half, rows), f32),
            pltpu.VMEM((2, pieces, packed_rows, lanes), f32),
            pltpu.VMEM((2, half, 2 * lanes), f32),
            pltpu.VMEM((2, 3 * half, 2 * lanes), bf16),
            pltpu.VMEM((2, half, 2 * lanes), f32),
            pltpu.VMEM((2, half, 2 * lanes), f32),
            pltpu.VMEM((2, half, rows), f32),
            pltpu.VMEM((2, half, rows), f32),
            pltpu.VMEM((2, width + HALO, rows), f32),
            pltpu.VMEM((packed_rows, rows), f32),
            pltpu.VMEM(phase.shape, f32),
            pltpu.VMEM(direction.shape, f32),
            dma((6,)),
            dma((3, mod_count - 1)),
            dma((3, mod_count - 1)),
            dma((8,)),
            dma((8,)),
            dma((mod_count - 1,)),
            dma((mod_count - 1,)),
            dma((everyone - 1,)),
            dma((everyone - 1,)),
            pltpu.SemaphoreType.REGULAR((max(tm_count - 1, 1), 2)),
        ],
        compiler_params=pltpu.CompilerParams(collective_id=0, has_side_effects=True),
    )(
        phase,
        direction,
        mod_tilts.reshape(1, 1),
        pupil_mask,
        wind_codes,
        noise_weight,
        jnp.asarray(coupling_tables(pupil, pieces)),
    )
    return pl.pallas_call(
        functools.partial(gather_kernel, float(frames * tm_count * pupil * rows)),
        out_shape=(jax.ShapeDtypeStruct(phase.shape, f32), jax.ShapeDtypeStruct((1,), f32)),
        in_specs=[vmem, vmem, vmem],
        out_specs=(vmem, smem),
    )(*[pltpu.with_memory_space_constraint(item, pltpu.VMEM) for item in sums])


def device_program(phase, direction, pupil_mask, mod_tilts, wind_codes, noise_weight):
    frames, width, rows = phase.shape
    mod_count = lax.axis_size("mod")
    fits = mod_count % frames == 0 and mod_tilts.shape[0] == 1 and frames > 1
    if fits:
        pieces = mod_count // frames
        fits = (
            lax.axis_size("tm") > 1
            and pieces % 2 == 0
            and rows == 128
            and rows % pieces == 0
            and width % (pieces * TILE) == 0
            and pieces & (pieces - 1) == 0
        )
    run = fused_device if fits else per_device
    return run(phase, direction, pupil_mask, mod_tilts, wind_codes, noise_weight)


def solution(mesh):
    return jax.shard_map(
        device_program,
        mesh=mesh,
        in_specs=(
            P(("grp", "tm"), "mod", None),
            P(("grp", "tm"), "mod", None),
            P(),
            P("mod"),
            P("grp", None),
            P(("grp", "tm"), None, None),
        ),
        out_specs=(P(("grp", "tm"), "mod", None), P("grp")),
        check_vma=False,
    )
```
